256 devices in a mesh: trade: 16 (over x_hi, y, core), scen: 16 (over x_lo, z).
Axes of the slice: x: 4 (x_hi: 2, x_lo: 2; x = x_hi * 2 + x_lo), y: 4, z: 8, core: 2. Of those that a mesh axis runs over, the one named last changes fastest.
Arguments:
- loadings: bfloat16 [200, 512, 1024], P(None, ('trade', 'scen')), may hold values from -0.4375 to 0.4375
- base_coef: bfloat16 [512, 1024], P(('trade', 'scen')), may hold values from -3 to 3
- shocks: float32 [32, 200], P('scen'), may hold values from -6 to 6
- scen_class: int32 [32], P('scen'), may hold values from 0 to 4, as said below
- names: int32 [256, 2], P('trade'), may hold values from 0 to 511, as said below
- trade_kind: int32 [256], P('trade'), may hold values from 0 to 1
- call_start: int32 [256], P('trade'), may hold values from 8 to 39
- knock_start: int32 [256], P('trade'), may hold values from 0 to 31
- offsets: int32 [256], P('trade'), may hold values from 0 to 2047
- normal_table: float32 [64, 2048], replicated, may hold values from -5 to 5
- book_value: float32 [256], P('trade'), may hold values from 0.5 to 1.5
Outputs:
- trade_value: float32 [256, 32], P('trade', 'scen')
- desk_pnl: float32 [32], P('scen')
- shortfall: float32 [], replicated
The draws below stay inside these ranges and needn't reach their ends.
Inputs may be any that keep to these rules, and one draw needn't show every extreme that they name: names = owner * 32 + local with owner the index of trade that holds the underlying. The trades of one index of trade (rows t * 16 to (t + 1) * 16 - 1) name underlyings of one owner at most 4 times over both columns, and exactly 4 times for some owner. The two names of a trade differ. scen_class[s] differs from (5 s) // 32 by at most one; scenario 0 has class 0.
All inputs are finite; a program needn't handle non-finite values.
Results may differ from the reference program's by a relative error of at most 0.0003.
Values may be sent and summed in bfloat16 or wider, within the bound.
No kernel may reach another device: no remote copies, remote signals or barrier semaphores. Data moves between devices by JAX's collectives and lax.ppermute only.
A program may use at most 64 MiB of HBM per device.

```python
import math
import jax
import jax.numpy as jnp
from jax import lax

F = 200
MAT = 64
COEF = 16
TROWS = 2048
PATHS = 256
TR_DEV = 16
ES_TAIL = 4
S = 32
TRADES = 256
OWNED = 32
UNDERLYINGS = 512
MK = 1024
CAP = 4


def draw_scen_class(key, part):
    positions = jnp.arange(S, dtype=jnp.int32)
    nudge = jax.random.randint(key, (S,), -1, 2).astype(jnp.int32)
    nudge = jnp.where(positions == 0, 0, nudge)
    nudge = jnp.where(positions == S - 1, 1, nudge)
    return jnp.clip(5 * positions // S + nudge, 0, 4).astype(jnp.int32)


def draw_names(key, part):
    block_count = TRADES // TR_DEV
    leg_count = 2 * TR_DEV
    slot_count = block_count * CAP

    def one_block(block_key):
        key_owner, key_rank, key_shuffle, key_local = jax.random.split(block_key, 4)
        full_owner = jax.random.randint(key_owner, (), 0, block_count)
        slot_rank = jax.random.permutation(key_rank, slot_count).astype(jnp.int32)
        slot_ids = jnp.arange(slot_count, dtype=jnp.int32)
        slot_rank = jnp.where(slot_ids // CAP == full_owner, slot_ids % CAP - CAP, slot_rank)
        chosen = jnp.argsort(slot_rank)[:leg_count].astype(jnp.int32)
        owner_ids = chosen // CAP
        owner_ids = owner_ids[jax.random.permutation(key_shuffle, leg_count)]
        local_ids = jax.random.randint(key_local, (leg_count,), 0, OWNED)
        owner_pair = owner_ids.reshape(TR_DEV, 2)
        local_pair = local_ids.reshape(TR_DEV, 2)
        clash = (owner_pair[:, 0] == owner_pair[:, 1]) & (local_pair[:, 0] == local_pair[:, 1])
        second_local = jnp.where(clash, (local_pair[:, 1] + 1) % OWNED, local_pair[:, 1])
        local_pair = jnp.stack([local_pair[:, 0], second_local], axis=1)
        return owner_pair * OWNED + local_pair
    block_keys = jax.random.split(key, block_count)
    return jax.vmap(one_block)(block_keys).reshape(TRADES, 2).astype(jnp.int32)


def with_ends(entries, stream_key, low, largest):
    place = [jax.random.randint(jax.random.fold_in(stream_key, axis), (), 0, length) for axis, length in enumerate(entries.shape)]
    longest = entries.shape.index(max(entries.shape))
    beside = place[:longest] + [(place[longest] + 1) % entries.shape[longest]] + place[longest + 1:]
    return entries.at[tuple(place)].set(low).at[tuple(beside)].set(largest)


def levels(own_key, dims, shards, low, high):
    def one(axis_at, shards_of):
        heights = jax.random.uniform(jax.random.fold_in(jax.random.fold_in(own_key, 6), axis_at), (shards_of,), jnp.float32, low / len(shards), high / len(shards))
        return jnp.repeat(jnp.exp(heights), dims[axis_at] // shards_of).reshape((-1,) + (1,) * (len(dims) - axis_at - 1))

    factor_of = one(*shards[0])
    for cut in shards[1:]:
        factor_of = factor_of * one(*cut)
    return factor_of


def gaussian(key, dims, deviation, reach, cuts=(), kind=jnp.bfloat16):
    values = deviation * jax.random.normal(key, dims, jnp.float32)
    if cuts:
        values = values * levels(key, dims, cuts, -0.22, 0.18)
    return jnp.clip(values, -reach, reach).astype(kind)


def setup_inputs(seed: int = 0) -> dict:
    keys = jax.random.split(jax.random.key(seed), 12)
    return {
        "loadings": gaussian(keys[0], (F, UNDERLYINGS, MK), F ** -0.5, 0.4375, ((1, 256),)),
        "base_coef": gaussian(keys[1], (UNDERLYINGS, MK), 0.5, 3.0, ((0, 256),)),
        "shocks": gaussian(keys[2], (S, F), 1.0, 6.0, ((0, 16),), jnp.float32),
        "scen_class": draw_scen_class(jax.random.fold_in(keys[11], 71), 0),
        "names": draw_names(jax.random.fold_in(keys[11], 71), 0),
        "trade_kind": with_ends(jax.random.randint(keys[5], (TRADES,), 0, 2), jax.random.fold_in(keys[5], 1), 0, 1).astype(jnp.int32),
        "call_start": with_ends(jax.random.randint(keys[6], (TRADES,), MAT // 8, MAT * 5 // 8), jax.random.fold_in(keys[6], 1), MAT // 8, (MAT * 5 // 8) - 1).astype(jnp.int32),
        "knock_start": with_ends(jax.random.randint(keys[7], (TRADES,), 0, MAT // 2), jax.random.fold_in(keys[7], 1), 0, (MAT // 2) - 1).astype(jnp.int32),
        "offsets": with_ends(jax.random.randint(keys[8], (TRADES,), 0, TROWS), jax.random.fold_in(keys[8], 1), 0, TROWS - 1).astype(jnp.int32),
        "normal_table": gaussian(keys[9], (MAT, TROWS), 1.0, 5.0, (), jnp.float32),
        "book_value": jnp.clip(0.5 + 1.0 * jax.random.uniform(keys[10], (TRADES,), jnp.float32) ** levels(keys[10], (TRADES,), ((0, 16),), -0.2, 0.2), 0.5, 1.5),
    }


CORRELATION = 0.6
CORR_COMPLEMENT = 0.8
BARRIER_LOG = -0.35
SMOOTHING = 0.03
COUPON_RATE = 0.08

def local_vol(coefficients, log_level):
    bent = jnp.tanh(log_level)
    cheb_prev = jnp.ones_like(bent)
    cheb_now = bent
    argument = coefficients[..., 0][..., None] * cheb_prev + coefficients[..., 1][..., None] * cheb_now
    for degree in range(2, coefficients.shape[-1]):
        cheb_next = 2.0 * bent * cheb_now - cheb_prev
        argument = argument + coefficients[..., degree][..., None] * cheb_next
        cheb_prev, cheb_now = (cheb_now, cheb_next)
    return 0.05 + 0.45 * jax.nn.sigmoid(argument)

def advance(path_state, step_index, draw_first, draw_other, coef_first, coef_second, call_start, knock_start, steps):
    logs_first, logs_second, survival, alive_share, paid_value = path_state
    step_size = 1.0 / steps
    root_step = math.sqrt(step_size)
    vol_first = local_vol(coef_first, logs_first)
    vol_second = local_vol(coef_second, logs_second)
    shock_first = draw_first[:, None, :]
    shock_second = (CORRELATION * draw_first + CORR_COMPLEMENT * draw_other)[:, None, :]
    logs_first = logs_first - 0.5 * vol_first * vol_first * step_size + vol_first * root_step * shock_first
    logs_second = logs_second - 0.5 * vol_second * vol_second * step_size + vol_second * root_step * shock_second
    worst_log = jnp.minimum(logs_first, logs_second)
    watched = (step_index >= knock_start)[:, None, None]
    survival = jnp.where(watched, survival * (1.0 - jax.nn.sigmoid((BARRIER_LOG - worst_log) / SMOOTHING)), survival)
    call_gap = steps // 8
    observed = ((step_index >= call_start) & ((step_index - call_start) % call_gap == 0) & (step_index < steps - 1))[:, None, None]
    call_prob = jax.nn.sigmoid(worst_log / SMOOTHING)
    coupon = 1.0 + COUPON_RATE * (step_index + 1).astype(jnp.float32) / steps
    paid_value = jnp.where(observed, paid_value + alive_share * call_prob * coupon, paid_value)
    alive_share = jnp.where(observed, alive_share * (1.0 - call_prob), alive_share)
    return (logs_first, logs_second, survival, alive_share, paid_value)

def settle(path_state, trade_kind):
    logs_first, logs_second, survival, alive_share, paid_value = path_state
    worst_log = jnp.minimum(logs_first, logs_second)
    knocked = 1.0 - survival
    growth = jnp.exp(worst_log)
    note_value = paid_value + alive_share * (1.0 + knocked * jnp.minimum(growth - 1.0, 0.0))
    put_value = knocked * jnp.maximum(1.0 - growth, 0.0)
    payoff = jnp.where((trade_kind == 0)[:, None, None], note_value, put_value)
    return lax.optimization_barrier(jnp.mean(payoff, axis=-1))

def horizon_scale(class_ids):
    table = jnp.sqrt(jnp.array([1.0, 2.0, 4.0, 6.0, 12.0], jnp.float32))
    hits = class_ids[:, None] == jnp.arange(5, dtype=jnp.int32)[None, :]
    return lax.optimization_barrier(jnp.sum(jnp.where(hits, table[None, :], 0.0), axis=1))

def reference(loadings, base_coef, shocks, scen_class, names, trade_kind, call_start, knock_start, offsets, normal_table, book_value):
    factors = shocks.shape[1]
    bucket = jnp.arange(factors, dtype=jnp.int32) * 5 // factors
    masked = jnp.where(bucket[None, :] >= scen_class[:, None], shocks, 0.0).astype(jnp.bfloat16)
    flat = jnp.dot(masked, loadings.reshape(factors, -1), preferred_element_type=jnp.float32)
    flat = flat + base_coef.reshape(1, -1).astype(jnp.float32)
    surface = flat.astype(jnp.bfloat16).reshape(S, UNDERLYINGS, MAT, COEF)
    coef_first = surface[:, names[:, 0]].astype(jnp.float32).transpose(2, 1, 0, 3)
    coef_second = surface[:, names[:, 1]].astype(jnp.float32).transpose(2, 1, 0, 3)
    row_index = (offsets[:, None] + jnp.arange(PATHS, dtype=jnp.int32)[None, :]) % TROWS
    draw_first = normal_table[:, row_index]
    draw_other = normal_table[:, (row_index + TROWS // 2) % TROWS]
    zeros = jnp.zeros((TRADES, S, PATHS), jnp.float32)
    ones = jnp.ones((TRADES, S, PATHS), jnp.float32)
    start_state = (zeros, zeros, ones, ones, zeros)

    def scan_step(path_state, inputs):
        step_index, first_now, other_now, coef_a, coef_b = inputs
        return (advance(path_state, step_index, first_now, other_now, coef_a, coef_b, call_start, knock_start, MAT), None)
    final_state, _ = lax.scan(scan_step, start_state, (jnp.arange(MAT, dtype=jnp.int32), draw_first, draw_other, coef_first, coef_second))
    trade_value = settle(final_state, trade_kind)
    desk_pnl = lax.optimization_barrier(jnp.sum(trade_value - book_value[:, None], axis=0)) / math.sqrt(TRADES)
    losses = -desk_pnl * horizon_scale(scen_class)
    shortfall = jnp.mean(lax.top_k(losses, ES_TAIL)[0])
    return (trade_value, desk_pnl, shortfall)
```

```python
import math

import jax
import jax.numpy as jnp
import numpy as np
from jax import lax
from jax.experimental import pallas as pl
from jax.experimental.pallas import tpu as pltpu
from jax.sharding import PartitionSpec as P

MAT = 64
COEF = 16
TROWS = 2048
PATHS = 256
ES_TAIL = 4


CORRELATION = 0.6
CORR_COMPLEMENT = 0.8
BARRIER_LOG = -0.35
SMOOTHING = 0.03
COUPON_RATE = 0.08


def joined_along(pieces, dim):
    pieces = jnp.moveaxis(pieces, 0, dim)
    lengths = pieces.shape
    return pieces.reshape(*lengths[:dim], lengths[dim] * lengths[dim + 1], *lengths[dim + 2 :])


def copy_for_each(array, axis):
    copies = jnp.broadcast_to(array, (lax.axis_size(axis), *array.shape))
    return lax.all_to_all(copies, axis, split_axis=0, concat_axis=0, tiled=True)


def gather_directly(array, axis, dim):
    return joined_along(copy_for_each(array, axis), dim)


def of_everyone(array, axis):
    return copy_for_each(array, axis).sum(axis=0)


def combined_pairwise(pieces, combine):
    while len(jax.tree.leaves(pieces)[0]) > 1:
        pieces = jax.vmap(combine)(*(pieces[side::2] for side in (0, 1)))
    return pieces[0]


def joined_all(array, axis, combine):
    pieces = copy_for_each(array, axis)
    return combined_pairwise(pieces, combine)


def power_basis():
    half = COEF // 2
    cheb = np.zeros((half, half))
    cheb[0, 0] = 1.0
    cheb[1, 1] = 1.0
    for k in range(2, half):
        cheb[k, 1:] = 2.0 * cheb[k - 1, :-1]
        cheb[k] -= cheb[k - 2]
    odd = np.zeros((half, half))
    odd[0, 0] = 1.0
    for k in range(1, half):
        odd[k] = 2.0 * cheb[k] - odd[k - 1]
    scale = 2.0 ** np.arange(half)
    conv = np.zeros((COEF, COEF))
    for k in range(half):
        conv[:half, 2 * k] = 0.5 * cheb[k] * scale
        conv[half:, 2 * k + 1] = 0.5 * odd[k] * scale
    return conv


def basis_block():
    return np.kron(np.eye(128 // COEF), power_basis())


def draws_kernel(offsets_ref, table_ref, out_ref, first_ref, second_ref, windows_ref):
    trades = offsets_ref.shape[0]
    root_step = math.sqrt(1.0 / MAT)
    table = table_ref[...]
    far = jnp.concatenate([table[:, TROWS // 2 :], table[:, : TROWS // 2]], axis=1)
    first = root_step * table
    second = root_step * (CORRELATION * table + CORR_COMPLEMENT * far)
    first_ref[:, :TROWS] = first
    first_ref[:, TROWS:] = first[:, :256]
    second_ref[:, :TROWS] = second
    second_ref[:, TROWS:] = second[:, :256]
    low = lax.broadcasted_iota(jnp.int32, (MAT, 128), 1) < 64

    def one_trade(trade, carry):
        offset = offsets_ref[trade]
        base = pl.multiple_of((offset // 128) * 128, 128)
        shift = offset % 128
        near = first_ref[:, pl.ds(base, 384)]
        other = second_ref[:, pl.ds(base, 384)]
        near_at = pltpu.roll(near, 384 - shift, 1)
        near_up = pltpu.roll(near, 320 - shift, 1)
        other_at = pltpu.roll(other, 384 - shift, 1)
        other_down = pltpu.roll(other, (448 - shift) % 384, 1)
        for half in range(2):
            cut = slice(half * 128, half * 128 + 128)
            even = jnp.where(low, near_at[:, cut], other_down[:, cut])
            odd = jnp.where(low, near_up[:, cut], other_at[:, cut])
            row = pl.multiple_of((2 * half * trades + trade) * MAT, MAT)
            windows_ref[pl.ds(row, MAT), :] = even
            row = pl.multiple_of(((2 * half + 1) * trades + trade) * MAT, MAT)
            windows_ref[pl.ds(row, MAT), :] = odd
        return carry

    lax.fori_loop(0, trades, one_trade, 0)

    def one_step(step, carry):
        rows = windows_ref[pl.ds(step, 4 * trades, stride=MAT), :]
        pieces = []
        for group in range(4):
            part = rows[group * trades : (group + 1) * trades]
            pieces += [part, part]
        out_ref[step] = jnp.concatenate(pieces, axis=0).T
        return carry

    lax.fori_loop(0, MAT, one_step, 0)


def path_draws(offsets, normal_table):
    trades = offsets.shape[0]
    return pl.pallas_call(
        draws_kernel,
        out_shape=jax.ShapeDtypeStruct((MAT, 128, 128), jnp.float32),
        in_specs=[
            pl.BlockSpec(memory_space=pltpu.SMEM),
            pl.BlockSpec(memory_space=pltpu.VMEM),
        ],
        out_specs=pl.BlockSpec(memory_space=pltpu.VMEM),
        scratch_shapes=[
            pltpu.VMEM((MAT, TROWS + 256), jnp.float32),
            pltpu.VMEM((MAT, TROWS + 256), jnp.float32),
            pltpu.VMEM((4 * trades * MAT, 128), jnp.float32),
        ],
        name="path_draws",
    )(offsets, normal_table)


BLOCK = 16
TILES = 4


def spread(ref, row):
    return ref[pl.ds(row, 8, stride=0), :]


def paths_kernel(rows_ref, pick_ref, basis_ref, terms_ref, draws_ref, out_ref, coef_ref, state_ref):
    block = pl.program_id(0)

    @pl.when(block == 0)
    def _():
        width = rows_ref.shape[1] // 2
        rows = jnp.concatenate([rows_ref[:, :width], rows_ref[:, width:]], axis=0)
        lane = lax.broadcasted_iota(jnp.int32, (128, 128), 1)
        for leg in range(2):
            pick = jnp.where(lane == pick_ref[:, leg : leg + 1], 1.0, 0.0).astype(jnp.bfloat16)
            chosen = jnp.dot(pick, rows, preferred_element_type=jnp.float32).astype(jnp.bfloat16)
            for part in range(width // 128):
                at = leg * width + part * 128
                coef_ref[at : at + 128, :] = lax.dot_general(
                    basis_ref[...],
                    chosen[:, part * 128 : part * 128 + 128],
                    (((1,), (1,)), ((), ())),
                    preferred_element_type=jnp.float32,
                )
        zeros = jnp.zeros((64, 128), jnp.float32)
        state_ref[0] = zeros
        state_ref[1] = zeros
        state_ref[2] = zeros + 1.0
        state_ref[3] = zeros + 1.0
        state_ref[4] = zeros

    step_size = 1.0 / MAT
    half_count = COEF // 2
    knock_start = spread(terms_ref, 0)
    call_start = spread(terms_ref, 1)
    slope = 0.5 / SMOOTHING
    barrier_shift = -BARRIER_LOG * slope

    def leg_step(logs, leg, step, draw_row):
        row = leg * (MAT * COEF) + step * COEF
        bent = [jnp.tanh(x) for x in logs]
        power = [y * y - 0.5 for y in bent]

        def series(first):
            top = spread(coef_ref, row + first + half_count - 1)
            total = [top] * len(logs)
            for k in range(half_count - 2, -1, -1):
                term = spread(coef_ref, row + first + k)
                total = [s * v + term for s, v in zip(total, power)]
            return total

        even = series(0)
        odd = series(half_count)
        out = []
        for at, x in enumerate(logs):
            vol = 0.275 + 0.225 * jnp.tanh(even[at] + bent[at] * odd[at])
            draw = draws_ref[step % BLOCK, pl.ds(draw_row + at * 8, 8), :]
            out.append(x + vol * (draw - (0.5 * step_size) * vol))
        return out

    for sweep in range(8 // TILES):
        top_row = sweep * TILES * 8

        def load(at):
            return [state_ref[at, top_row + i * 8 : top_row + i * 8 + 8, :] for i in range(TILES)]

        def one_step(step, state):
            first, second, survival, alive, paid = state
            first = leg_step(first, 0, step, top_row)
            second = leg_step(second, 1, step, 64 + top_row)
            worst = [jnp.minimum(a, b) for a, b in zip(first, second)]
            scaled = [w * slope for w in worst]
            watch = jnp.where(step >= knock_start, barrier_shift, 1e6)
            gap = step - call_start
            seen = (gap >= 0) & ((gap & (MAT // 8 - 1)) == 0) & (step < MAT - 1)
            call = jnp.where(seen, 0.0, -1e6)
            coupon = 1.0 + COUPON_RATE * (step + 1).astype(jnp.float32) / MAT
            survival = [
                v * (0.5 + 0.5 * jnp.tanh(w + watch)) for v, w in zip(survival, scaled)
            ]
            called = [a * (0.5 + 0.5 * jnp.tanh(w + call)) for a, w in zip(alive, scaled)]
            paid = [p + c * coupon for p, c in zip(paid, called)]
            alive = [a - c for a, c in zip(alive, called)]
            return (first, second, survival, alive, paid)

        def some_steps(at, state):
            for inner in range(UNROLL):
                state = one_step(block * BLOCK + at * UNROLL + inner, state)
            return state

        state = tuple(load(at) for at in range(5))
        state = lax.fori_loop(0, BLOCK // UNROLL, some_steps, state)
        for at in range(5):
            for i in range(TILES):
                state_ref[at, top_row + i * 8 : top_row + i * 8 + 8, :] = state[at][i]

    @pl.when(block == MAT // BLOCK - 1)
    def _():
        worst = jnp.minimum(state_ref[0], state_ref[1])
        knocked = 1.0 - state_ref[2]
        growth = jnp.exp(worst)
        note = state_ref[4] + state_ref[3] * (1.0 + knocked * jnp.minimum(growth - 1.0, 0.0))
        put = knocked * jnp.maximum(1.0 - growth, 0.0)
        payoff = jnp.where(terms_ref[2:3, :] == 0, note, put)
        total = jnp.sum(payoff, axis=0, keepdims=True)
        total = jnp.broadcast_to(total, (8, 128))
        total = total + pltpu.roll(total, 64, 1)
        total = total + pltpu.roll(total, 32, 1)
        out_ref[...] = total * (1.0 / PATHS)


UNROLL = 4


def path_values(rows, pick, terms, draws):
    whole = lambda *dims: pl.BlockSpec(dims, lambda b: (0,) * len(dims))
    return pl.pallas_call(
        paths_kernel,
        grid=(MAT // BLOCK,),
        out_shape=jax.ShapeDtypeStruct((8, 128), jnp.float32),
        in_specs=[
            whole(*rows.shape),
            whole(*pick.shape),
            whole(128, 128),
            whole(*terms.shape),
            pl.BlockSpec((BLOCK, 128, 128), lambda b: (b, 0, 0)),
        ],
        out_specs=whole(8, 128),
        scratch_shapes=[
            pltpu.VMEM((2 * MAT * COEF + 8, 128), jnp.float32),
            pltpu.VMEM((5, 64, 128), jnp.float32),
        ],
        name="path_values",
    )(rows, pick, jnp.asarray(basis_block(), jnp.bfloat16), terms, draws)


def horizon_scale(class_ids):
    table = jnp.sqrt(jnp.array([1.0, 2.0, 4.0, 6.0, 12.0], jnp.float32))
    hits = class_ids[:, None] == jnp.arange(5, dtype=jnp.int32)[None, :]
    return jnp.sum(jnp.where(hits, table[None, :], 0.0), axis=1)


def keep_worst(first_set, second_set):
    return lax.top_k(jnp.concatenate([first_set, second_set]), first_set.shape[0])[0]


def per_device(
    loadings,
    base_coef,
    shocks,
    scen_class,
    names,
    trade_kind,
    call_start,
    knock_start,
    offsets,
    normal_table,
    book_value,
):
    factors = shocks.shape[1]
    scen_here = shocks.shape[0]
    trades_here = names.shape[0]
    bucket = jnp.arange(factors, dtype=jnp.int32) * 5 // factors
    masked = jnp.where(bucket[None, :] >= scen_class[:, None], shocks, 0.0).astype(jnp.bfloat16)
    everyone = gather_directly(masked, "scen", 0)
    product = jnp.einsum("sf,fum->usm", everyone, loadings, preferred_element_type=jnp.float32)
    own_coef = (product + base_coef[:, None, :].astype(jnp.float32)).astype(jnp.bfloat16)
    owned = lax.all_to_all(own_coef, "scen", split_axis=1, concat_axis=0, tiled=True)
    owned_rows = owned.shape[0]
    row_width = owned.shape[1] * owned.shape[2]
    coef_rows = owned.reshape(owned_rows, row_width)
    leg_names = names.reshape(-1)
    leg_total = leg_names.shape[0]
    width_trade = lax.axis_size("trade")
    cap_slots = max(2, (4 * trades_here + width_trade - 1) // width_trade)
    owner_row = leg_names // owned_rows
    local_row = leg_names % owned_rows
    leg_ids = jnp.arange(leg_total, dtype=jnp.int32)
    same_owner = (owner_row[None, :] == owner_row[:, None]) & (leg_ids[None, :] < leg_ids[:, None])
    slot_rank = jnp.sum(same_owner.astype(jnp.int32), axis=1)
    owner_match = (
        owner_row[None, None, :] == jnp.arange(width_trade, dtype=jnp.int32)[:, None, None]
    )
    slot_match = slot_rank[None, None, :] == jnp.arange(cap_slots, dtype=jnp.int32)[None, :, None]
    wanted_rows = jnp.sum(jnp.where(owner_match & slot_match, local_row[None, None, :], 0), axis=2)
    fetched = coef_rows[
        lax.all_to_all(wanted_rows, "trade", split_axis=0, concat_axis=0, tiled=True)
    ]
    replies = lax.all_to_all(fetched, "trade", split_axis=0, concat_axis=0, tiled=True)
    draws = path_draws(offsets, normal_table)
    lanes = 128 // trades_here
    slot = (owner_row * cap_slots + slot_rank).reshape(trades_here, 2)
    scen_of = (jnp.arange(128, dtype=jnp.int32) // trades_here) % scen_here
    pick = jnp.tile(slot, (lanes, 1)) + (scen_of * (width_trade * cap_slots))[:, None]
    terms = jnp.tile(jnp.stack([knock_start, call_start, trade_kind]), (1, lanes))
    terms = jnp.concatenate([terms, jnp.zeros((13, 128), jnp.int32)])
    values = path_values(replies.reshape(width_trade * cap_slots, row_width), pick, terms, draws)
    trade_value = values[0, : scen_here * trades_here].reshape(scen_here, trades_here).T
    partial_pnl = jnp.sum(trade_value - book_value[:, None], axis=0)
    total_pnl = of_everyone(partial_pnl, "trade")
    desk_pnl = total_pnl / math.sqrt(trades_here * lax.axis_size("trade"))
    losses = -desk_pnl * horizon_scale(scen_class)
    candidates = jnp.concatenate([losses, jnp.full((ES_TAIL,), -1e30, jnp.float32)])
    local_tail = lax.top_k(candidates, ES_TAIL)[0]
    merged_tail = joined_all(local_tail, "scen", keep_worst)
    shortfall = jnp.mean(merged_tail)
    return (trade_value, desk_pnl, shortfall)


def solution(mesh):
    return jax.shard_map(
        per_device,
        mesh=mesh,
        in_specs=(
            P(None, ("trade", "scen"), None),
            P(("trade", "scen"), None),
            P("scen", None),
            P("scen"),
            P("trade", None),
            P("trade"),
            P("trade"),
            P("trade"),
            P("trade"),
            P(),
            P("trade"),
        ),
        out_specs=(P("trade", "scen"), P("scen"), P()),
        check_vma=False,
    )
```

```python
import math

import jax
import jax.numpy as jnp
import numpy as np
from jax import lax
from jax.experimental import pallas as pl
from jax.experimental.pallas import tpu as pltpu
from jax.sharding import PartitionSpec as P

MAT = 64
COEF = 16
TROWS = 2048
PATHS = 256
ES_TAIL = 4


CORRELATION = 0.6
CORR_COMPLEMENT = 0.8
BARRIER_LOG = -0.35
SMOOTHING = 0.03
COUPON_RATE = 0.08


def spread_to_all(array, axes):
    copies = jnp.broadcast_to(array, (lax.axis_size(axes), *array.shape))
    return lax.all_to_all(copies, axes, split_axis=0, concat_axis=0, tiled=True)


def power_basis():
    half = COEF // 2
    cheb = np.zeros((half, half))
    cheb[0, 0] = 1.0
    cheb[1, 1] = 1.0
    for k in range(2, half):
        cheb[k, 1:] = 2.0 * cheb[k - 1, :-1]
        cheb[k] -= cheb[k - 2]
    odd = np.zeros((half, half))
    odd[0, 0] = 1.0
    for k in range(1, half):
        odd[k] = 2.0 * cheb[k] - odd[k - 1]
    scale = 2.0 ** np.arange(half)
    conv = np.zeros((COEF, COEF))
    for k in range(half):
        conv[:half, 2 * k] = 0.5 * cheb[k] * scale
        conv[half:, 2 * k + 1] = 0.5 * odd[k] * scale
    return conv


def basis_block():
    return np.kron(np.eye(128 // COEF), power_basis())


def draws_kernel(offsets_ref, table_ref, out_ref, first_ref, second_ref, windows_ref):
    trades = offsets_ref.shape[0]
    root_step = math.sqrt(1.0 / MAT)
    table = table_ref[...]
    far = jnp.concatenate([table[:, TROWS // 2 :], table[:, : TROWS // 2]], axis=1)
    first = root_step * table
    second = root_step * (CORRELATION * table + CORR_COMPLEMENT * far)
    first_ref[:, :TROWS] = first
    first_ref[:, TROWS:] = first[:, :256]
    second_ref[:, :TROWS] = second
    second_ref[:, TROWS:] = second[:, :256]
    low = lax.broadcasted_iota(jnp.int32, (MAT, 128), 1) < 64

    def one_trade(trade, carry):
        offset = offsets_ref[trade]
        base = pl.multiple_of((offset // 128) * 128, 128)
        shift = offset % 128
        near = first_ref[:, pl.ds(base, 384)]
        other = second_ref[:, pl.ds(base, 384)]
        near_at = pltpu.roll(near, 384 - shift, 1)
        near_up = pltpu.roll(near, 320 - shift, 1)
        other_at = pltpu.roll(other, 384 - shift, 1)
        other_down = pltpu.roll(other, (448 - shift) % 384, 1)
        for half in range(2):
            cut = slice(half * 128, half * 128 + 128)
            even = jnp.where(low, near_at[:, cut], other_down[:, cut])
            odd = jnp.where(low, near_up[:, cut], other_at[:, cut])
            row = pl.multiple_of((2 * half * trades + trade) * MAT, MAT)
            windows_ref[pl.ds(row, MAT), :] = even
            row = pl.multiple_of(((2 * half + 1) * trades + trade) * MAT, MAT)
            windows_ref[pl.ds(row, MAT), :] = odd
        return carry

    lax.fori_loop(0, trades, one_trade, 0)

    def one_step(step, carry):
        rows = windows_ref[pl.ds(step, 4 * trades, stride=MAT), :]
        pieces = []
        for group in range(4):
            part = rows[group * trades : (group + 1) * trades]
            pieces += [part, part]
        out_ref[step] = jnp.concatenate(pieces, axis=0).T
        return carry

    lax.fori_loop(0, MAT, one_step, 0)


def path_draws(offsets, normal_table):
    trades = offsets.shape[0]
    return pl.pallas_call(
        draws_kernel,
        out_shape=jax.ShapeDtypeStruct((MAT, 128, 128), jnp.float32),
        in_specs=[
            pl.BlockSpec(memory_space=pltpu.SMEM),
            pl.BlockSpec(memory_space=pltpu.VMEM),
        ],
        out_specs=pl.BlockSpec(memory_space=pltpu.VMEM),
        scratch_shapes=[
            pltpu.VMEM((MAT, TROWS + 256), jnp.float32),
            pltpu.VMEM((MAT, TROWS + 256), jnp.float32),
            pltpu.VMEM((4 * trades * MAT, 128), jnp.float32),
        ],
        name="path_draws",
    )(offsets, normal_table)


BLOCK = 16
TILES = 4


def spread(ref, row):
    return ref[pl.ds(row, 8, stride=0), :]


def paths_kernel(rows_ref, pick_ref, basis_ref, terms_ref, draws_ref, out_ref, coef_ref, state_ref):
    block = pl.program_id(0)

    @pl.when(block == 0)
    def _():
        width = rows_ref.shape[1] // 2
        rows = jnp.concatenate([rows_ref[:, :width], rows_ref[:, width:]], axis=0)
        lane = lax.broadcasted_iota(jnp.int32, (128, 128), 1)
        for leg in range(2):
            pick = jnp.where(lane == pick_ref[:, leg : leg + 1], 1.0, 0.0).astype(jnp.bfloat16)
            chosen = jnp.dot(pick, rows, preferred_element_type=jnp.float32).astype(jnp.bfloat16)
            for part in range(width // 128):
                at = leg * width + part * 128
                coef_ref[at : at + 128, :] = lax.dot_general(
                    basis_ref[...],
                    chosen[:, part * 128 : part * 128 + 128],
                    (((1,), (1,)), ((), ())),
                    preferred_element_type=jnp.float32,
                )
        zeros = jnp.zeros((64, 128), jnp.float32)
        state_ref[0] = zeros
        state_ref[1] = zeros
        state_ref[2] = zeros + 1.0
        state_ref[3] = zeros + 1.0
        state_ref[4] = zeros

    step_size = 1.0 / MAT
    half_count = COEF // 2
    knock_start = spread(terms_ref, 0)
    call_start = spread(terms_ref, 1)
    slope = 0.5 / SMOOTHING
    barrier_shift = -BARRIER_LOG * slope

    def leg_step(logs, leg, step, draw_row):
        row = leg * (MAT * COEF) + step * COEF
        bent = [jnp.tanh(x) for x in logs]
        power = [y * y - 0.5 for y in bent]

        def series(first):
            top = spread(coef_ref, row + first + half_count - 1)
            total = [top] * len(logs)
            for k in range(half_count - 2, -1, -1):
                term = spread(coef_ref, row + first + k)
                total = [s * v + term for s, v in zip(total, power)]
            return total

        even = series(0)
        odd = series(half_count)
        out = []
        for at, x in enumerate(logs):
            vol = 0.275 + 0.225 * jnp.tanh(even[at] + bent[at] * odd[at])
            draw = draws_ref[step % BLOCK, pl.ds(draw_row + at * 8, 8), :]
            out.append(x + vol * (draw - (0.5 * step_size) * vol))
        return out

    for sweep in range(8 // TILES):
        top_row = sweep * TILES * 8

        def load(at):
            return [state_ref[at, top_row + i * 8 : top_row + i * 8 + 8, :] for i in range(TILES)]

        def one_step(step, state):
            first, second, survival, alive, paid = state
            first = leg_step(first, 0, step, top_row)
            second = leg_step(second, 1, step, 64 + top_row)
            worst = [jnp.minimum(a, b) for a, b in zip(first, second)]
            scaled = [w * slope for w in worst]
            watch = jnp.where(step >= knock_start, barrier_shift, 1e6)
            gap = step - call_start
            seen = (gap >= 0) & ((gap & (MAT // 8 - 1)) == 0) & (step < MAT - 1)
            call = jnp.where(seen, 0.0, -1e6)
            coupon = 1.0 + COUPON_RATE * (step + 1).astype(jnp.float32) / MAT
            survival = [
                v * (0.5 + 0.5 * jnp.tanh(w + watch)) for v, w in zip(survival, scaled)
            ]
            called = [a * (0.5 + 0.5 * jnp.tanh(w + call)) for a, w in zip(alive, scaled)]
            paid = [p + c * coupon for p, c in zip(paid, called)]
            alive = [a - c for a, c in zip(alive, called)]
            return (first, second, survival, alive, paid)

        def some_steps(at, state):
            for inner in range(UNROLL):
                state = one_step(block * BLOCK + at * UNROLL + inner, state)
            return state

        state = tuple(load(at) for at in range(5))
        state = lax.fori_loop(0, BLOCK // UNROLL, some_steps, state)
        for at in range(5):
            for i in range(TILES):
                state_ref[at, top_row + i * 8 : top_row + i * 8 + 8, :] = state[at][i]

    @pl.when(block == MAT // BLOCK - 1)
    def _():
        worst = jnp.minimum(state_ref[0], state_ref[1])
        knocked = 1.0 - state_ref[2]
        growth = jnp.exp(worst)
        note = state_ref[4] + state_ref[3] * (1.0 + knocked * jnp.minimum(growth - 1.0, 0.0))
        put = knocked * jnp.maximum(1.0 - growth, 0.0)
        payoff = jnp.where(terms_ref[2:3, :] == 0, note, put)
        total = jnp.sum(payoff, axis=0, keepdims=True)
        total = jnp.broadcast_to(total, (8, 128))
        total = total + pltpu.roll(total, 64, 1)
        total = total + pltpu.roll(total, 32, 1)
        out_ref[...] = total * (1.0 / PATHS)


UNROLL = 4


def path_values(rows, pick, terms, draws):
    whole = lambda *dims: pl.BlockSpec(dims, lambda b: (0,) * len(dims))
    return pl.pallas_call(
        paths_kernel,
        grid=(MAT // BLOCK,),
        out_shape=jax.ShapeDtypeStruct((8, 128), jnp.float32),
        in_specs=[
            whole(*rows.shape),
            whole(*pick.shape),
            whole(128, 128),
            whole(*terms.shape),
            pl.BlockSpec((BLOCK, 128, 128), lambda b: (b, 0, 0)),
        ],
        out_specs=whole(8, 128),
        scratch_shapes=[
            pltpu.VMEM((2 * MAT * COEF + 8, 128), jnp.float32),
            pltpu.VMEM((5, 64, 128), jnp.float32),
        ],
        name="path_values",
    )(rows, pick, jnp.asarray(basis_block(), jnp.bfloat16), terms, draws)


def horizon_scale(class_ids):
    table = jnp.sqrt(jnp.array([1.0, 2.0, 4.0, 6.0, 12.0], jnp.float32))
    hits = class_ids[:, None] == jnp.arange(5, dtype=jnp.int32)[None, :]
    return jnp.sum(jnp.where(hits, table[None, :], 0.0), axis=1)


def per_device(
    loadings,
    base_coef,
    shocks,
    scen_class,
    names,
    trade_kind,
    call_start,
    knock_start,
    offsets,
    normal_table,
    book_value,
):
    factors = shocks.shape[1]
    scen_here = shocks.shape[0]
    trades_here = names.shape[0]
    width_trade = lax.axis_size("trade")
    width_scen = lax.axis_size("scen")
    trade_at = lax.axis_index("trade")
    scen_at = lax.axis_index("scen")
    everywhere = ("trade", "scen")
    owned_rows = base_coef.shape[0] * width_scen
    cap_slots = max(2, (4 * trades_here + width_trade - 1) // width_trade)

    bucket = jnp.arange(factors, dtype=jnp.int32) * 5 // factors
    masked = jnp.where(bucket[None, :] >= scen_class[:, None], shocks, 0.0)
    slice_len = 16 * (-(-factors // (16 * width_trade)))
    masked = jnp.pad(masked, ((0, 0), (0, slice_len * width_trade - factors)))
    shock_part = lax.dynamic_slice_in_dim(masked, trade_at * slice_len, slice_len, axis=1)
    leg_names = names.reshape(-1)
    leg_total = leg_names.shape[0]
    leg_len = leg_total // width_scen
    leg_part = lax.dynamic_slice_in_dim(leg_names, scen_at * leg_len, leg_len)
    parts = [
        shock_part.reshape(-1),
        (leg_part // owned_rows).astype(jnp.float32),
        (leg_part % owned_rows).astype(jnp.float32),
        scen_class.astype(jnp.float32),
    ]
    sent = jnp.concatenate(parts).astype(jnp.bfloat16)
    heard = spread_to_all(sent[None, :], everywhere)
    heard = heard.reshape(width_trade, width_scen, sent.shape[0])
    shock_len = scen_here * slice_len
    everyone = heard[:, :, :shock_len].reshape(width_trade, width_scen, scen_here, slice_len)
    everyone = everyone.transpose(1, 2, 0, 3).reshape(width_scen * scen_here, -1)[:, :factors]
    owner_all = heard[:, :, shock_len : shock_len + leg_len].reshape(width_trade, leg_total)
    local_all = heard[:, :, shock_len + leg_len : shock_len + 2 * leg_len]
    local_all = local_all.reshape(width_trade, leg_total).astype(jnp.int32)
    class_all = heard[0, :, shock_len + 2 * leg_len :].astype(jnp.int32).reshape(-1)

    product = jnp.einsum("sf,fum->usm", everyone, loadings, preferred_element_type=jnp.float32)
    own_coef = (product + base_coef[:, None, :].astype(jnp.float32)).astype(jnp.bfloat16)
    draws = path_draws(offsets, normal_table)
    own_coef, draws = lax.optimization_barrier((own_coef, draws))
    owned = lax.all_to_all(own_coef, "scen", split_axis=1, concat_axis=0, tiled=True)
    row_width = owned.shape[1] * owned.shape[2]
    coef_rows = owned.reshape(owned_rows, row_width)

    leg_ids = jnp.arange(leg_total, dtype=jnp.int32)
    earlier = leg_ids[None, :] < leg_ids[:, None]
    mine = owner_all.astype(jnp.int32) == trade_at
    rank_here = jnp.sum((mine[:, None, :] & earlier[None]).astype(jnp.int32), axis=2)
    slots = jnp.arange(cap_slots, dtype=jnp.int32)
    hit = mine[:, None, :] & (rank_here[:, None, :] == slots[None, :, None])
    wanted = jnp.sum(jnp.where(hit, local_all[:, None, :], 0), axis=2)
    fetched = coef_rows[wanted]
    replies = lax.all_to_all(fetched, "trade", split_axis=0, concat_axis=0, tiled=True)

    owner_row = leg_names // owned_rows
    same_owner = (owner_row[None, :] == owner_row[:, None]) & earlier
    slot_rank = jnp.sum(same_owner.astype(jnp.int32), axis=1)
    lanes = 128 // trades_here
    slot = (owner_row * cap_slots + slot_rank).reshape(trades_here, 2)
    scen_of = (jnp.arange(128, dtype=jnp.int32) // trades_here) % scen_here
    pick = jnp.tile(slot, (lanes, 1)) + (scen_of * (width_trade * cap_slots))[:, None]
    terms = jnp.tile(jnp.stack([knock_start, call_start, trade_kind]), (1, lanes))
    terms = jnp.concatenate([terms, jnp.zeros((13, 128), jnp.int32)])
    values = path_values(replies.reshape(width_trade * cap_slots, row_width), pick, terms, draws)
    trade_value = values[0, : scen_here * trades_here].reshape(scen_here, trades_here).T

    partial_pnl = jnp.sum(trade_value - book_value[:, None], axis=0)
    parts_all = spread_to_all(partial_pnl[None, :], everywhere)
    parts_all = parts_all.reshape(width_trade, width_scen * scen_here)
    pnl_all = jnp.sum(parts_all, axis=0) / math.sqrt(trades_here * width_trade)
    desk_pnl = lax.dynamic_slice_in_dim(pnl_all, scen_at * scen_here, scen_here)
    losses = -pnl_all * horizon_scale(class_all)
    shortfall = jnp.mean(lax.top_k(losses, ES_TAIL)[0])
    return (trade_value, desk_pnl, shortfall)


def solution(mesh):
    return jax.shard_map(
        per_device,
        mesh=mesh,
        in_specs=(
            P(None, ("trade", "scen"), None),
            P(("trade", "scen"), None),
            P("scen", None),
            P("scen"),
            P("trade", None),
            P("trade"),
            P("trade"),
            P("trade"),
            P("trade"),
            P(),
            P("trade"),
        ),
        out_specs=(P("trade", "scen"), P("scen"), P()),
        check_vma=False,
    )
```

```python
import math

import jax
import jax.numpy as jnp
import numpy as np
from jax import lax
from jax.experimental import pallas as pl
from jax.experimental.pallas import tpu as pltpu
from jax.sharding import PartitionSpec as P

MAT = 64
COEF = 16
TROWS = 2048
PATHS = 256
ES_TAIL = 4


CORRELATION = 0.6
CORR_COMPLEMENT = 0.8
BARRIER_LOG = -0.35
SMOOTHING = 0.03
COUPON_RATE = 0.08


def power_basis():
    half = COEF // 2
    cheb = np.zeros((half, half))
    cheb[0, 0] = 1.0
    cheb[1, 1] = 1.0
    for k in range(2, half):
        cheb[k, 1:] = 2.0 * cheb[k - 1, :-1]
        cheb[k] -= cheb[k - 2]
    odd = np.zeros((half, half))
    odd[0, 0] = 1.0
    for k in range(1, half):
        odd[k] = 2.0 * cheb[k] - odd[k - 1]
    scale = 2.0 ** np.arange(half)
    conv = np.zeros((COEF, COEF))
    for k in range(half):
        conv[:half, 2 * k] = 0.5 * cheb[k] * scale
        conv[half:, 2 * k + 1] = 0.5 * odd[k] * scale
    return conv


def basis_block():
    return np.kron(np.eye(128 // COEF), power_basis())


def windows_kernel(offsets_ref, table_ref, windows_ref, first_ref, second_ref):
    trades = offsets_ref.shape[0]
    root_step = math.sqrt(1.0 / MAT)
    table = table_ref[...]
    far = jnp.concatenate([table[:, TROWS // 2 :], table[:, : TROWS // 2]], axis=1)
    first = root_step * table
    second = root_step * (CORRELATION * table + CORR_COMPLEMENT * far)
    first_ref[:, :TROWS] = first
    first_ref[:, TROWS:] = first[:, :256]
    second_ref[:, :TROWS] = second
    second_ref[:, TROWS:] = second[:, :256]
    low = lax.broadcasted_iota(jnp.int32, (MAT, 128), 1) < 64

    def one_trade(trade, carry):
        offset = offsets_ref[trade]
        base = pl.multiple_of((offset // 128) * 128, 128)
        shift = offset % 128
        near = first_ref[:, pl.ds(base, 384)]
        other = second_ref[:, pl.ds(base, 384)]
        near_at = pltpu.roll(near, 384 - shift, 1)
        near_up = pltpu.roll(near, 320 - shift, 1)
        other_at = pltpu.roll(other, 384 - shift, 1)
        other_down = pltpu.roll(other, (448 - shift) % 384, 1)
        for half in range(2):
            cut = slice(half * 128, half * 128 + 128)
            even = jnp.where(low, near_at[:, cut], other_down[:, cut])
            odd = jnp.where(low, near_up[:, cut], other_at[:, cut])
            row = pl.multiple_of((2 * half * trades + trade) * MAT, MAT)
            windows_ref[pl.ds(row, MAT), :] = even
            row = pl.multiple_of(((2 * half + 1) * trades + trade) * MAT, MAT)
            windows_ref[pl.ds(row, MAT), :] = odd
        return carry

    lax.fori_loop(0, trades, one_trade, 0)


def path_windows(offsets, normal_table):
    trades = offsets.shape[0]
    return pl.pallas_call(
        windows_kernel,
        out_shape=jax.ShapeDtypeStruct((4 * trades * MAT, 128), jnp.float32),
        in_specs=[
            pl.BlockSpec(memory_space=pltpu.SMEM),
            pl.BlockSpec(memory_space=pltpu.VMEM),
        ],
        out_specs=pl.BlockSpec(memory_space=pltpu.VMEM),
        scratch_shapes=[
            pltpu.VMEM((MAT, TROWS + 256), jnp.float32),
            pltpu.VMEM((MAT, TROWS + 256), jnp.float32),
        ],
        name="path_windows",
    )(offsets, normal_table)


TURN = 8


def turn_kernel(first_step, windows_ref, *refs):
    out_ref = refs[-1]
    groups = windows_ref.shape[0] // MAT
    trades = groups // 4
    start = first_step + pl.program_id(0) * TURN
    for inner in range(TURN):
        rows = windows_ref[pl.ds(start + inner, groups, stride=MAT), :]
        pieces = []
        for group in range(4):
            part = rows[group * trades : (group + 1) * trades]
            pieces += [part, part]
        out_ref[inner] = jnp.concatenate(pieces, axis=0).T


def path_draws(windows, half, earlier=None):
    blocks = MAT // 2 // TURN
    operands = [windows] if earlier is None else [windows, earlier]
    in_specs = [pl.BlockSpec(windows.shape, lambda b: (0, 0)), pl.BlockSpec(memory_space=pl.ANY)]
    return pl.pallas_call(
        lambda *refs: turn_kernel(half * (MAT // 2), *refs),
        grid=(blocks,),
        out_shape=jax.ShapeDtypeStruct((MAT, 128, 128), jnp.float32),
        in_specs=in_specs[: len(operands)],
        out_specs=pl.BlockSpec((TURN, 128, 128), lambda b: (half * blocks + b, 0, 0)),
        input_output_aliases={} if earlier is None else {1: 0},
        name="path_draws",
    )(*operands)


BLOCK = 16
TILES = 4


def spread(ref, row):
    return ref[pl.ds(row, 8, stride=0), :]


def paths_kernel(
    rows_ref, pick_ref, basis_ref, terms_ref, book_ref, draws_ref,
    value_ref, sent_ref, coef_ref, state_ref,
):
    block = pl.program_id(0)

    @pl.when(block == 0)
    def _():
        width = rows_ref.shape[1] // 2
        rows = jnp.concatenate([rows_ref[:, :width], rows_ref[:, width:]], axis=0)
        lane = lax.broadcasted_iota(jnp.int32, (128, 128), 1)
        for leg in range(2):
            pick = jnp.where(lane == pick_ref[:, leg : leg + 1], 1.0, 0.0).astype(jnp.bfloat16)
            chosen = jnp.dot(pick, rows, preferred_element_type=jnp.float32).astype(jnp.bfloat16)
            for part in range(width // 128):
                at = leg * width + part * 128
                coef_ref[at : at + 128, :] = lax.dot_general(
                    basis_ref[...],
                    chosen[:, part * 128 : part * 128 + 128],
                    (((1,), (1,)), ((), ())),
                    preferred_element_type=jnp.float32,
                )
        zeros = jnp.zeros((64, 128), jnp.float32)
        state_ref[0] = zeros
        state_ref[1] = zeros
        state_ref[2] = zeros + 1.0
        state_ref[3] = zeros + 1.0
        state_ref[4] = zeros

    step_size = 1.0 / MAT
    half_count = COEF // 2
    knock_start = spread(terms_ref, 0)
    call_start = spread(terms_ref, 1)
    slope = 0.5 / SMOOTHING
    barrier_shift = -BARRIER_LOG * slope

    def leg_step(logs, leg, step, draw_row):
        row = leg * (MAT * COEF) + step * COEF
        bent = [jnp.tanh(x) for x in logs]
        power = [y * y - 0.5 for y in bent]

        def series(first):
            top = spread(coef_ref, row + first + half_count - 1)
            total = [top] * len(logs)
            for k in range(half_count - 2, -1, -1):
                term = spread(coef_ref, row + first + k)
                total = [s * v + term for s, v in zip(total, power)]
            return total

        even = series(0)
        odd = series(half_count)
        out = []
        for at, x in enumerate(logs):
            vol = 0.275 + 0.225 * jnp.tanh(even[at] + bent[at] * odd[at])
            draw = draws_ref[step % BLOCK, pl.ds(draw_row + at * 8, 8), :]
            out.append(x + vol * (draw - (0.5 * step_size) * vol))
        return out

    for sweep in range(8 // TILES):
        top_row = sweep * TILES * 8

        def load(at):
            return [state_ref[at, top_row + i * 8 : top_row + i * 8 + 8, :] for i in range(TILES)]

        def one_step(step, state):
            first, second, survival, alive, paid = state
            first = leg_step(first, 0, step, top_row)
            second = leg_step(second, 1, step, 64 + top_row)
            worst = [jnp.minimum(a, b) for a, b in zip(first, second)]
            scaled = [w * slope for w in worst]
            watch = jnp.where(step >= knock_start, barrier_shift, 1e6)
            gap = step - call_start
            seen = (gap >= 0) & ((gap & (MAT // 8 - 1)) == 0) & (step < MAT - 1)
            call = jnp.where(seen, 0.0, -1e6)
            coupon = 1.0 + COUPON_RATE * (step + 1).astype(jnp.float32) / MAT
            survival = [
                v * (0.5 + 0.5 * jnp.tanh(w + watch)) for v, w in zip(survival, scaled)
            ]
            called = [a * (0.5 + 0.5 * jnp.tanh(w + call)) for a, w in zip(alive, scaled)]
            paid = [p + c * coupon for p, c in zip(paid, called)]
            alive = [a - c for a, c in zip(alive, called)]
            return (first, second, survival, alive, paid)

        def some_steps(at, state):
            for inner in range(UNROLL):
                state = one_step(block * BLOCK + at * UNROLL + inner, state)
            return state

        state = tuple(load(at) for at in range(5))
        state = lax.fori_loop(0, BLOCK // UNROLL, some_steps, state)
        for at in range(5):
            for i in range(TILES):
                state_ref[at, top_row + i * 8 : top_row + i * 8 + 8, :] = state[at][i]

    @pl.when(block == MAT // BLOCK - 1)
    def _():
        worst = jnp.minimum(state_ref[0], state_ref[1])
        knocked = 1.0 - state_ref[2]
        growth = jnp.exp(worst)
        note = state_ref[4] + state_ref[3] * (1.0 + knocked * jnp.minimum(growth - 1.0, 0.0))
        put = knocked * jnp.maximum(1.0 - growth, 0.0)
        payoff = jnp.where(terms_ref[2:3, :] == 0, note, put)
        total = jnp.sum(payoff, axis=0, keepdims=True)
        total = jnp.broadcast_to(total, (8, 128))
        total = total + pltpu.roll(total, 64, 1)
        total = total + pltpu.roll(total, 32, 1)
        total = total * (1.0 / PATHS)
        trades = value_ref.shape[1]
        value_ref[0:1, :] = total[0:1, :trades]
        value_ref[1:2, :] = pltpu.roll(total, 128 - trades, 1)[0:1, :trades]
        gain = total - spread(book_ref, 0)
        shift = trades // 2
        while shift:
            gain = gain + pltpu.roll(gain, shift, 1)
            shift //= 2
        lane = lax.broadcasted_iota(jnp.int32, (8, 128), 1)
        sent = spread(book_ref, 1)
        sent = jnp.where(lane == 0, pltpu.roll(gain, 129 - trades, 1), sent)
        sent = jnp.where(lane == 1, pltpu.roll(gain, 130 - 2 * trades, 1), sent)
        sent_ref[...] = jnp.broadcast_to(sent[0:1, :], sent_ref.shape)


UNROLL = 4


def path_values(rows, pick, terms, book, draws, trades, devices):
    whole = lambda *dims: pl.BlockSpec(dims, lambda b: (0,) * len(dims))
    return pl.pallas_call(
        paths_kernel,
        grid=(MAT // BLOCK,),
        out_shape=(
            jax.ShapeDtypeStruct((2, trades), jnp.float32),
            jax.ShapeDtypeStruct((devices, 128), jnp.float32),
        ),
        in_specs=[
            whole(*rows.shape),
            whole(*pick.shape),
            whole(128, 128),
            whole(*terms.shape),
            whole(*book.shape),
            pl.BlockSpec((BLOCK, 128, 128), lambda b: (b, 0, 0)),
        ],
        out_specs=(whole(2, trades), whole(devices, 128)),
        scratch_shapes=[
            pltpu.VMEM((2 * MAT * COEF + 8, 128), jnp.float32),
            pltpu.VMEM((5, 64, 128), jnp.float32),
        ],
        name="path_values",
    )(rows, pick, jnp.asarray(basis_block(), jnp.bfloat16), terms, book, draws)


def horizon_scale(class_ids):
    table = jnp.sqrt(jnp.array([1.0, 2.0, 4.0, 6.0, 12.0], jnp.float32))
    hits = class_ids[:, None] == jnp.arange(5, dtype=jnp.int32)[None, :]
    return jnp.sum(jnp.where(hits, table[None, :], 0.0), axis=1)


SLICE = 16
LEG_LANE = 2 * SLICE


def pack_kernel(names_ref, class_ref, shocks_ref, out_ref, wide_ref):
    trade_at = lax.axis_index("trade")
    scen_at = lax.axis_index("scen")
    factors = shocks_ref.shape[1]
    wide = wide_ref.shape[1]
    wide_ref[...] = jnp.zeros(wide_ref.shape, jnp.float32)
    wide_ref[0:2, :factors] = shocks_ref[...]
    row = lax.broadcasted_iota(jnp.int32, wide_ref.shape, 0)
    lane = lax.broadcasted_iota(jnp.int32, wide_ref.shape, 1)
    class_of = jnp.where(row == 0, class_ref[0], class_ref[1])
    masked = jnp.where(lane * 5 >= class_of * factors, wide_ref[...], 0.0)
    here = pltpu.roll(masked, (wide - trade_at * SLICE) % wide, 1)[:, :128]
    after = pltpu.roll(here, SLICE, 1)
    lane = lax.broadcasted_iota(jnp.int32, (1, 128), 1)
    sent = jnp.where(lane < SLICE, here[0:1, :], after[1:2, :])
    for leg in range(2):
        name = names_ref[leg, scen_at].astype(jnp.float32)
        sent = jnp.where(lane == LEG_LANE + leg, name, sent)
    out_ref[...] = jnp.broadcast_to(sent, out_ref.shape)


def pack(names, scen_class, shocks, devices):
    return pl.pallas_call(
        pack_kernel,
        out_shape=jax.ShapeDtypeStruct((devices, 128), jnp.float32),
        in_specs=[
            pl.BlockSpec(memory_space=pltpu.SMEM),
            pl.BlockSpec(memory_space=pltpu.SMEM),
            pl.BlockSpec(memory_space=pltpu.VMEM),
        ],
        out_specs=pl.BlockSpec(memory_space=pltpu.VMEM),
        scratch_shapes=[pltpu.VMEM((8, 256), jnp.float32)],
        name="pack",
    )(names, scen_class, shocks)


def unpack_kernel(heard_ref, out_ref, rows_ref):
    scens = out_ref.shape[0] // 2
    lane = lax.broadcasted_iota(jnp.int32, (scens, 128), 1)
    per_tile = 128 // SLICE
    for tile in range(2):
        for scen in range(2):
            total = jnp.zeros((scens, 128), jnp.float32)
            for at in range(per_tile):
                first = (tile * per_tile + at) * scens
                part = heard_ref[first : first + scens, :]
                part = pltpu.roll(part, ((at - scen) * SLICE) % 128, 1)
                total = jnp.where(lane // SLICE == at, part, total)
            rows_ref[pl.ds(tile * 2 * scens + scen, scens, stride=2), :] = total
    out_ref[:, :128] = rows_ref[: 2 * scens, :].astype(jnp.bfloat16)
    out_ref[:, 128:] = rows_ref[2 * scens :, : out_ref.shape[1] - 128].astype(jnp.bfloat16)


def unpack(heard, scens, factors):
    return pl.pallas_call(
        unpack_kernel,
        out_shape=jax.ShapeDtypeStruct((2 * scens, factors), jnp.bfloat16),
        in_specs=[pl.BlockSpec(memory_space=pltpu.VMEM)],
        out_specs=pl.BlockSpec(memory_space=pltpu.VMEM),
        scratch_shapes=[pltpu.VMEM((4 * scens, 128), jnp.float32)],
        name="unpack",
    )(heard)


def tail_kernel(heard_ref, desk_ref, tail_ref):
    scen_at = lax.axis_index("scen")
    scens = lax.axis_size("scen")
    blocks = heard_ref.shape[0] // scens
    total = heard_ref[0:scens, :]
    factor = pltpu.roll(total, 64, 1)
    for block in range(1, blocks):
        total = total + heard_ref[block * scens : (block + 1) * scens, :]
    pnl = total / math.sqrt(blocks * 16)
    row = lax.broadcasted_iota(jnp.int32, (scens, 128), 0)
    lane = lax.broadcasted_iota(jnp.int32, (scens, 128), 1)
    order = (row * 128 + lane).astype(jnp.float32)
    low = -3e38
    loss = jnp.where(lane < 2, -pnl * factor, low)
    tail = 0.0
    for _ in range(ES_TAIL):
        worst = jnp.max(loss)
        place = jnp.min(jnp.where(loss == worst, order, 1e9))
        loss = jnp.where(order == place, low, loss)
        tail = tail + worst
    tail_ref[0] = tail * (1.0 / ES_TAIL)
    for scen in range(2):
        desk_ref[scen] = jnp.sum(jnp.where((row == scen_at) & (lane == scen), pnl, 0.0))


def tail(heard):
    return pl.pallas_call(
        tail_kernel,
        out_shape=(
            jax.ShapeDtypeStruct((2,), jnp.float32),
            jax.ShapeDtypeStruct((1,), jnp.float32),
        ),
        in_specs=[pl.BlockSpec(memory_space=pltpu.VMEM)],
        out_specs=(
            pl.BlockSpec(memory_space=pltpu.SMEM),
            pl.BlockSpec(memory_space=pltpu.SMEM),
        ),
        name="tail",
    )(heard)


def per_device(
    loadings,
    base_coef,
    shocks,
    scen_class,
    names,
    trade_kind,
    call_start,
    knock_start,
    offsets,
    normal_table,
    book_value,
):
    factors = shocks.shape[1]
    scen_here = shocks.shape[0]
    trades_here = names.shape[0]
    width_trade = lax.axis_size("trade")
    width_scen = lax.axis_size("scen")
    trade_at = lax.axis_index("trade")
    everywhere = ("trade", "scen")
    devices = width_trade * width_scen
    owned_rows = base_coef.shape[0] * width_scen
    cap_slots = max(2, (4 * trades_here + width_trade - 1) // width_trade)
    leg_total = 2 * trades_here

    sent = pack(names.T, scen_class, shocks, devices)
    heard = lax.all_to_all(sent, everywhere, split_axis=0, concat_axis=0, tiled=True)
    everyone = unpack(heard, width_scen, factors)
    product = jnp.einsum("sf,fum->usm", everyone, loadings, preferred_element_type=jnp.float32)
    own_coef = (product + base_coef[:, None, :].astype(jnp.float32)).astype(jnp.bfloat16)
    windows = path_windows(offsets, normal_table)
    own_coef, windows, heard = lax.optimization_barrier((own_coef, windows, heard))
    owned = lax.all_to_all(own_coef, "scen", split_axis=1, concat_axis=0, tiled=True)
    row_width = owned.shape[1] * owned.shape[2]
    coef_rows = owned.reshape(owned_rows, row_width)

    names_all = heard[:, LEG_LANE : LEG_LANE + 2].astype(jnp.int32).reshape(width_trade, leg_total)
    leg_ids = jnp.arange(leg_total, dtype=jnp.int32)
    earlier = leg_ids[None, :] < leg_ids[:, None]
    mine = names_all // owned_rows == trade_at
    local_all = names_all % owned_rows
    rank_here = jnp.sum((mine[:, None, :] & earlier[None]).astype(jnp.int32), axis=2)
    slots = jnp.arange(cap_slots, dtype=jnp.int32)
    hit = mine[:, None, :] & (rank_here[:, None, :] == slots[None, :, None])
    wanted = jnp.sum(jnp.where(hit, local_all[:, None, :], 0), axis=2)
    fetched = coef_rows[wanted]
    draws = path_draws(windows, 0)
    fetched, draws = lax.optimization_barrier((fetched, draws))
    replies = lax.all_to_all(fetched, "trade", split_axis=0, concat_axis=0, tiled=True)
    draws = path_draws(windows, 1, draws)

    owner_row = names.reshape(-1) // owned_rows
    same_owner = (owner_row[None, :] == owner_row[:, None]) & earlier
    slot_rank = jnp.sum(same_owner.astype(jnp.int32), axis=1)
    lanes = 128 // trades_here
    slot = (owner_row * cap_slots + slot_rank).reshape(trades_here, 2)
    scen_of = (jnp.arange(128, dtype=jnp.int32) // trades_here) % scen_here
    pick = jnp.tile(slot, (lanes, 1)) + (scen_of * (width_trade * cap_slots))[:, None]
    terms = jnp.tile(jnp.stack([knock_start, call_start, trade_kind]), (1, lanes))
    terms = jnp.concatenate([terms, jnp.zeros((13, 128), jnp.int32)])
    factor_row = jnp.pad(horizon_scale(scen_class), (64, 64 - scen_here))
    book = jnp.stack([jnp.tile(book_value, lanes), factor_row])
    book = jnp.concatenate([book, jnp.zeros((14, 128), jnp.float32)])
    rows = replies.reshape(width_trade * cap_slots, row_width)
    values, parts = path_values(rows, pick, terms, book, draws, trades_here, devices)
    parts = lax.all_to_all(parts, everywhere, split_axis=0, concat_axis=0, tiled=True)
    desk_pnl, shortfall = tail(parts)
    return (values.T, desk_pnl, shortfall[0])


def solution(mesh):
    return jax.shard_map(
        per_device,
        mesh=mesh,
        in_specs=(
            P(None, ("trade", "scen"), None),
            P(("trade", "scen"), None),
            P("scen", None),
            P("scen"),
            P("trade", None),
            P("trade"),
            P("trade"),
            P("trade"),
            P("trade"),
            P(),
            P("trade"),
        ),
        out_specs=(P("trade", "scen"), P("scen"), P()),
        check_vma=False,
    )
```

```python
import functools
import math

import jax
import jax.numpy as jnp
import numpy as np
from jax import lax
from jax.experimental import pallas as pl
from jax.experimental.pallas import tpu as pltpu
from jax.sharding import PartitionSpec as P

MAT = 64
COEF = 16
TROWS = 2048
PATHS = 256
ES_TAIL = 4


CORRELATION = 0.6
CORR_COMPLEMENT = 0.8
BARRIER_LOG = -0.35
SMOOTHING = 0.03
COUPON_RATE = 0.08


VOL_LOW = 0.05
VOL_SPAN = 0.225


def power_basis():
    half = COEF // 2
    cheb = np.zeros((half, half))
    cheb[0, 0] = 1.0
    cheb[1, 1] = 1.0
    for k in range(2, half):
        cheb[k, 1:] = 2.0 * cheb[k - 1, :-1]
        cheb[k] -= cheb[k - 2]
    odd = np.zeros((half, half))
    odd[0, 0] = 1.0
    for k in range(1, half):
        odd[k] = 2.0 * cheb[k] - odd[k - 1]
    scale = 2.0 ** np.arange(half)
    conv = np.zeros((COEF, COEF))
    for k in range(half):
        conv[:half, 2 * k] = 0.5 * cheb[k] * scale
        conv[half:, 2 * k + 1] = 0.5 * odd[k] * scale
    return conv


def basis_block():
    return np.kron(np.eye(128 // COEF), power_basis())


def label_rows(names_ref, class_ref, knock_ref, call_ref, kind_ref, book_ref, count_ref, owned_rows, cap_slots):
    trades = knock_ref.shape[0]
    owners = count_ref.shape[0]
    lane = lax.broadcasted_iota(jnp.int32, (1, 128), 1)
    trade_of = lane % trades
    for owner in range(owners):
        count_ref[owner] = 0
    rows = [jnp.zeros((1, 128), jnp.int32)] * 5
    book = jnp.zeros((1, 128), jnp.float32)
    for trade in range(trades):
        here = trade_of == trade
        scalars = [knock_ref[trade], call_ref[trade], kind_ref[trade]]
        for leg in range(2):
            owner = names_ref[leg, trade] // owned_rows
            rank = count_ref[owner]
            count_ref[owner] = rank + 1
            scalars.append(owner * cap_slots + rank)
        rows = [jnp.where(here, x, row) for x, row in zip(scalars, rows)]
        book = jnp.where(here, book_ref[trade], book)
    scen_shift = jnp.where((lane // trades) % 2 == 1, owners * cap_slots, 0)
    rows = rows[:3] + [row + scen_shift for row in rows[3:]]
    class_of = jnp.where(lane == 64, class_ref[0], jnp.where(lane == 65, class_ref[1], -1))
    factor = jnp.zeros((1, 128), jnp.float32)
    for at, weeks in enumerate((1.0, 2.0, 4.0, 6.0, 12.0)):
        factor = jnp.where(class_of == at, math.sqrt(weeks), factor)
    return rows, [book, factor]


def windows_kernel(
    offsets_ref, names_ref, class_ref, knock_ref, call_ref, kind_ref, book_ref, table_ref,
    windows_ref, terms_ref, amounts_ref, first_ref, second_ref, count_ref, *, owned_rows, cap_slots,
):
    rows, amounts = label_rows(
        names_ref, class_ref, knock_ref, call_ref, kind_ref, book_ref, count_ref, owned_rows, cap_slots
    )
    for at, row in enumerate(rows):
        terms_ref[at : at + 1, :] = row
    for at, row in enumerate(amounts):
        amounts_ref[at : at + 1, :] = row
    trades = offsets_ref.shape[0]
    root_step = VOL_SPAN * math.sqrt(1.0 / MAT)
    table = table_ref[...]
    far = jnp.concatenate([table[:, TROWS // 2 :], table[:, : TROWS // 2]], axis=1)
    first = root_step * table
    second = root_step * (CORRELATION * table + CORR_COMPLEMENT * far)
    first_ref[:, :TROWS] = first
    first_ref[:, TROWS:] = first[:, :256]
    second_ref[:, :TROWS] = second
    second_ref[:, TROWS:] = second[:, :256]
    low = lax.broadcasted_iota(jnp.int32, (MAT, 128), 1) < 64

    def one_trade(trade, carry):
        offset = offsets_ref[trade]
        base = pl.multiple_of((offset // 128) * 128, 128)
        shift = offset % 128
        near = first_ref[:, pl.ds(base, 384)]
        other = second_ref[:, pl.ds(base, 384)]
        near_at = pltpu.roll(near, 384 - shift, 1)
        near_up = pltpu.roll(near, 320 - shift, 1)
        other_at = pltpu.roll(other, 384 - shift, 1)
        other_down = pltpu.roll(other, (448 - shift) % 384, 1)
        for half in range(2):
            cut = slice(half * 128, half * 128 + 128)
            even = jnp.where(low, near_at[:, cut], other_down[:, cut])
            odd = jnp.where(low, near_up[:, cut], other_at[:, cut])
            row = pl.multiple_of((2 * half * trades + trade) * MAT, MAT)
            windows_ref[pl.ds(row, MAT), :] = even
            row = pl.multiple_of(((2 * half + 1) * trades + trade) * MAT, MAT)
            windows_ref[pl.ds(row, MAT), :] = odd
        return carry

    lax.fori_loop(0, trades, one_trade, 0)


def path_windows(offsets, names, scen_class, knock, call, kind, book, table, owners, owned_rows, cap_slots):
    trades = offsets.shape[0]
    scalars = pl.BlockSpec(memory_space=pltpu.SMEM)
    vector = pl.BlockSpec(memory_space=pltpu.VMEM)
    return pl.pallas_call(
        functools.partial(windows_kernel, owned_rows=owned_rows, cap_slots=cap_slots),
        out_shape=(
            jax.ShapeDtypeStruct((4 * trades * MAT, 128), jnp.float32),
            jax.ShapeDtypeStruct((16, 128), jnp.int32),
            jax.ShapeDtypeStruct((16, 128), jnp.float32),
        ),
        in_specs=[scalars] * 7 + [vector],
        out_specs=(vector, vector, vector),
        scratch_shapes=[
            pltpu.VMEM((MAT, TROWS + 256), jnp.float32),
            pltpu.VMEM((MAT, TROWS + 256), jnp.float32),
            pltpu.SMEM((owners,), jnp.int32),
        ],
        name="path_windows",
    )(offsets, names, scen_class, knock, call, kind, book, table)


TURN = 8


def turn_kernel(first_step, windows_ref, *refs):
    out_ref = refs[-1]
    groups = windows_ref.shape[0] // MAT
    trades = groups // 4
    start = first_step + pl.program_id(0) * TURN
    for inner in range(TURN):
        rows = windows_ref[pl.ds(start + inner, groups, stride=MAT), :]
        pieces = []
        for group in range(4):
            part = rows[group * trades : (group + 1) * trades]
            pieces += [part, part]
        out_ref[inner] = jnp.concatenate(pieces, axis=0).T


def path_draws(windows, half, earlier=None):
    blocks = MAT // 2 // TURN
    operands = [windows] if earlier is None else [windows, earlier]
    in_specs = [pl.BlockSpec(windows.shape, lambda b: (0, 0)), pl.BlockSpec(memory_space=pl.ANY)]
    return pl.pallas_call(
        lambda *refs: turn_kernel(half * (MAT // 2), *refs),
        grid=(blocks,),
        out_shape=jax.ShapeDtypeStruct((MAT, 128, 128), jnp.float32),
        in_specs=in_specs[: len(operands)],
        out_specs=pl.BlockSpec((TURN, 128, 128), lambda b: (half * blocks + b, 0, 0)),
        input_output_aliases={} if earlier is None else {1: 0},
        name="path_draws",
    )(*operands)


BLOCK = 16
TILES = 4


def spread(ref, row):
    return ref[pl.ds(row, 8, stride=0), :]


def paths_kernel(
    rows_ref, basis_ref, terms_ref, book_ref, draws_ref,
    value_ref, sent_ref, coef_ref, state_ref,
):
    block = pl.program_id(0)

    @pl.when(block == 0)
    def _():
        width = rows_ref.shape[1] // 2
        rows = jnp.concatenate([rows_ref[:, :width], rows_ref[:, width:]], axis=0)
        slot = lax.broadcasted_iota(jnp.int32, (128, 128), 0)
        for leg in range(2):
            pick = jnp.where(slot == terms_ref[3 + leg : 4 + leg, :], 1.0, 0.0)
            pick = pick.T.astype(jnp.bfloat16)
            chosen = jnp.dot(pick, rows, preferred_element_type=jnp.float32).astype(jnp.bfloat16)
            for part in range(width // 128):
                at = leg * width + part * 128
                coef_ref[at : at + 128, :] = lax.dot_general(
                    basis_ref[...],
                    chosen[:, part * 128 : part * 128 + 128],
                    (((1,), (1,)), ((), ())),
                    preferred_element_type=jnp.float32,
                )
        zeros = jnp.zeros((64, 128), jnp.float32)
        state_ref[0] = zeros
        state_ref[1] = zeros
        state_ref[2] = zeros + 1.0
        state_ref[3] = zeros + 1.0
        state_ref[4] = zeros

    step_size = 1.0 / MAT
    half_count = COEF // 2
    knock_start = spread(terms_ref, 0)
    call_start = spread(terms_ref, 1)
    slope = 0.5 / SMOOTHING
    barrier_shift = -BARRIER_LOG * slope

    def leg_step(logs, leg, step, draw_row):
        row = leg * (MAT * COEF) + step * COEF
        bent = [jnp.tanh(x) for x in logs]
        power = [y * y - 0.5 for y in bent]

        def series(first):
            top = spread(coef_ref, row + first + half_count - 1)
            total = [top] * len(logs)
            for k in range(half_count - 2, -1, -1):
                term = spread(coef_ref, row + first + k)
                total = [s * v + term for s, v in zip(total, power)]
            return total

        even = series(0)
        odd = series(half_count)
        out = []
        for at, x in enumerate(logs):
            vol = VOL_LOW / VOL_SPAN + 1.0 + jnp.tanh(even[at] + bent[at] * odd[at])
            draw = draws_ref[step % BLOCK, pl.ds(draw_row + at * 8, 8), :]
            out.append(x + vol * (draw - (0.5 * step_size * VOL_SPAN**2) * vol))
        return out

    for sweep in range(8 // TILES):
        top_row = sweep * TILES * 8

        def load(at):
            return [state_ref[at, top_row + i * 8 : top_row + i * 8 + 8, :] for i in range(TILES)]

        def one_step(step, state):
            first, second, survival, alive, paid = state
            first = leg_step(first, 0, step, top_row)
            second = leg_step(second, 1, step, 64 + top_row)
            worst = [jnp.minimum(a, b) for a, b in zip(first, second)]
            scaled = [w * slope for w in worst]
            watch = jnp.where(step >= knock_start, barrier_shift, 1e6)
            gap = step - call_start
            seen = (gap >= 0) & ((gap & (MAT // 8 - 1)) == 0) & (step < MAT - 1)
            call = jnp.where(seen, 0.0, -1e6)
            passed = step % BLOCK
            coupon = 1.0 + COUPON_RATE * (step + 1).astype(jnp.float32) / MAT
            coupon = coupon * (1 << (BLOCK - 1 - passed)).astype(jnp.float32) * 2.0**-BLOCK
            survival = [v + v * jnp.tanh(w + watch) for v, w in zip(survival, scaled)]
            part = [a * jnp.tanh(w + call) for a, w in zip(alive, scaled)]
            paid = [p + (a + c) * coupon for p, a, c in zip(paid, alive, part)]
            alive = [a - c for a, c in zip(alive, part)]
            return (first, second, survival, alive, paid)

        def some_steps(at, state):
            for inner in range(UNROLL):
                state = one_step(block * BLOCK + at * UNROLL + inner, state)
            return state

        state = tuple(load(at) for at in range(5))
        state = lax.fori_loop(0, BLOCK // UNROLL, some_steps, state)
        for at in range(5):
            for i in range(TILES):
                value = state[at][i] * 2.0**-BLOCK if at in (2, 3) else state[at][i]
                state_ref[at, top_row + i * 8 : top_row + i * 8 + 8, :] = value

    @pl.when(block == MAT // BLOCK - 1)
    def _():
        worst = jnp.minimum(state_ref[0], state_ref[1])
        knocked = 1.0 - state_ref[2]
        growth = jnp.exp(worst)
        note = state_ref[4] + state_ref[3] * (1.0 + knocked * jnp.minimum(growth - 1.0, 0.0))
        put = knocked * jnp.maximum(1.0 - growth, 0.0)
        payoff = jnp.where(terms_ref[2:3, :] == 0, note, put)
        total = jnp.sum(payoff, axis=0, keepdims=True)
        total = jnp.broadcast_to(total, (8, 128))
        total = total + pltpu.roll(total, 64, 1)
        total = total + pltpu.roll(total, 32, 1)
        total = total * (1.0 / PATHS)
        trades = value_ref.shape[1]
        value_ref[0:1, :] = total[0:1, :trades]
        value_ref[1:2, :] = pltpu.roll(total, 128 - trades, 1)[0:1, :trades]
        gain = total - spread(book_ref, 0)
        shift = trades // 2
        while shift:
            gain = gain + pltpu.roll(gain, shift, 1)
            shift //= 2
        lane = lax.broadcasted_iota(jnp.int32, (8, 128), 1)
        sent = spread(book_ref, 1)
        sent = jnp.where(lane == 0, pltpu.roll(gain, 129 - trades, 1), sent)
        sent = jnp.where(lane == 1, pltpu.roll(gain, 130 - 2 * trades, 1), sent)
        sent_ref[...] = jnp.broadcast_to(sent[0:1, :], sent_ref.shape)


UNROLL = 4


def path_values(rows, terms, book, draws, trades, devices):
    whole = lambda *dims: pl.BlockSpec(dims, lambda b: (0,) * len(dims))
    return pl.pallas_call(
        paths_kernel,
        grid=(MAT // BLOCK,),
        out_shape=(
            jax.ShapeDtypeStruct((2, trades), jnp.float32),
            jax.ShapeDtypeStruct((devices, 128), jnp.float32),
        ),
        in_specs=[
            whole(*rows.shape),
            whole(128, 128),
            whole(*terms.shape),
            whole(*book.shape),
            pl.BlockSpec((BLOCK, 128, 128), lambda b: (b, 0, 0)),
        ],
        out_specs=(whole(2, trades), whole(devices, 128)),
        scratch_shapes=[
            pltpu.VMEM((2 * MAT * COEF + 8, 128), jnp.float32),
            pltpu.VMEM((5, 64, 128), jnp.float32),
        ],
        name="path_values",
    )(rows, jnp.asarray(basis_block(), jnp.bfloat16), terms, book, draws)


SLICE = 16
LEG_LANE = 2 * SLICE


def pack_kernel(names_ref, class_ref, shocks_ref, out_ref, wide_ref):
    trade_at = lax.axis_index("trade")
    scen_at = lax.axis_index("scen")
    factors = shocks_ref.shape[1]
    wide = wide_ref.shape[1]
    wide_ref[...] = jnp.zeros(wide_ref.shape, jnp.float32)
    wide_ref[0:2, :factors] = shocks_ref[...]
    row = lax.broadcasted_iota(jnp.int32, wide_ref.shape, 0)
    lane = lax.broadcasted_iota(jnp.int32, wide_ref.shape, 1)
    class_of = jnp.where(row == 0, class_ref[0], class_ref[1])
    masked = jnp.where(lane * 5 >= class_of * factors, wide_ref[...], 0.0)
    here = pltpu.roll(masked, (wide - trade_at * SLICE) % wide, 1)[:, :128]
    after = pltpu.roll(here, SLICE, 1)
    lane = lax.broadcasted_iota(jnp.int32, (1, 128), 1)
    sent = jnp.where(lane < SLICE, here[0:1, :], after[1:2, :])
    for leg in range(2):
        name = names_ref[leg, scen_at].astype(jnp.float32)
        sent = jnp.where(lane == LEG_LANE + leg, name, sent)
    out_ref[...] = jnp.broadcast_to(sent, out_ref.shape)


def pack(names, scen_class, shocks, devices):
    return pl.pallas_call(
        pack_kernel,
        out_shape=jax.ShapeDtypeStruct((devices, 128), jnp.float32),
        in_specs=[
            pl.BlockSpec(memory_space=pltpu.SMEM),
            pl.BlockSpec(memory_space=pltpu.SMEM),
            pl.BlockSpec(memory_space=pltpu.VMEM),
        ],
        out_specs=pl.BlockSpec(memory_space=pltpu.VMEM),
        scratch_shapes=[pltpu.VMEM((8, 256), jnp.float32)],
        name="pack",
    )(names, scen_class, shocks)


def unpack_kernel(heard_ref, out_ref, rows_ref):
    scens = out_ref.shape[0] // 2
    lane = lax.broadcasted_iota(jnp.int32, (scens, 128), 1)
    per_tile = 128 // SLICE
    for tile in range(2):
        for scen in range(2):
            total = jnp.zeros((scens, 128), jnp.float32)
            for at in range(per_tile):
                first = (tile * per_tile + at) * scens
                part = heard_ref[first : first + scens, :]
                part = pltpu.roll(part, ((at - scen) * SLICE) % 128, 1)
                total = jnp.where(lane // SLICE == at, part, total)
            rows_ref[pl.ds(tile * 2 * scens + scen, scens, stride=2), :] = total
    out_ref[:, :128] = rows_ref[: 2 * scens, :].astype(jnp.bfloat16)
    out_ref[:, 128:] = rows_ref[2 * scens :, : out_ref.shape[1] - 128].astype(jnp.bfloat16)


def unpack(heard, scens, factors):
    return pl.pallas_call(
        unpack_kernel,
        out_shape=jax.ShapeDtypeStruct((2 * scens, factors), jnp.bfloat16),
        in_specs=[pl.BlockSpec(memory_space=pltpu.VMEM)],
        out_specs=pl.BlockSpec(memory_space=pltpu.VMEM),
        scratch_shapes=[pltpu.VMEM((4 * scens, 128), jnp.float32)],
        name="unpack",
    )(heard)


def tail_kernel(heard_ref, desk_ref, tail_ref):
    scen_at = lax.axis_index("scen")
    scens = lax.axis_size("scen")
    blocks = heard_ref.shape[0] // scens
    total = heard_ref[0:scens, :]
    factor = pltpu.roll(total, 64, 1)
    for block in range(1, blocks):
        total = total + heard_ref[block * scens : (block + 1) * scens, :]
    pnl = total / math.sqrt(blocks * 16)
    row = lax.broadcasted_iota(jnp.int32, (scens, 128), 0)
    lane = lax.broadcasted_iota(jnp.int32, (scens, 128), 1)
    loss = -pnl * factor
    turned = jnp.concatenate([loss] * (128 // scens), axis=0).T
    other = lane % scens
    picked = jnp.zeros((1, 128), jnp.float32)
    for scen in range(2):
        mine = turned[scen : scen + 1, :]
        above = jnp.zeros((scens, 128), jnp.float32)
        for rival in range(2):
            theirs = jnp.broadcast_to(loss[:, rival : rival + 1], (scens, 128))
            first = 2 * row + rival < 2 * other + scen
            above = above + jnp.where((theirs > mine) | ((theirs == mine) & first), 1.0, 0.0)
        rank = jnp.sum(above, axis=0, keepdims=True)
        picked = picked + jnp.where((rank < ES_TAIL) & (lane[0:1] < scens), mine, 0.0)
    tail_ref[0] = jnp.sum(picked) * (1.0 / ES_TAIL)
    for scen in range(2):
        desk_ref[scen] = jnp.sum(jnp.where((row == scen_at) & (lane == scen), pnl, 0.0))


def tail(heard):
    return pl.pallas_call(
        tail_kernel,
        out_shape=(
            jax.ShapeDtypeStruct((2,), jnp.float32),
            jax.ShapeDtypeStruct((1,), jnp.float32),
        ),
        in_specs=[pl.BlockSpec(memory_space=pltpu.VMEM)],
        out_specs=(
            pl.BlockSpec(memory_space=pltpu.SMEM),
            pl.BlockSpec(memory_space=pltpu.SMEM),
        ),
        name="tail",
    )(heard)


def per_device(
    loadings,
    base_coef,
    shocks,
    scen_class,
    names,
    trade_kind,
    call_start,
    knock_start,
    offsets,
    normal_table,
    book_value,
):
    factors = shocks.shape[1]
    scen_here = shocks.shape[0]
    trades_here = names.shape[0]
    width_trade = lax.axis_size("trade")
    width_scen = lax.axis_size("scen")
    trade_at = lax.axis_index("trade")
    everywhere = ("trade", "scen")
    devices = width_trade * width_scen
    owned_rows = base_coef.shape[0] * width_scen
    cap_slots = max(2, (4 * trades_here + width_trade - 1) // width_trade)
    leg_total = 2 * trades_here

    sent = pack(names.T, scen_class, shocks, devices)
    heard = lax.all_to_all(sent, everywhere, split_axis=0, concat_axis=0, tiled=True)
    everyone = unpack(heard, width_scen, factors)
    product = jnp.einsum("sf,fum->usm", everyone, loadings, preferred_element_type=jnp.float32)
    own_coef = (product + base_coef[:, None, :].astype(jnp.float32)).astype(jnp.bfloat16)
    windows, terms, book = path_windows(
        offsets, names.T, scen_class, knock_start, call_start, trade_kind, book_value,
        normal_table, width_trade, owned_rows, cap_slots,
    )
    own_coef, windows, heard = lax.optimization_barrier((own_coef, windows, heard))
    owned = lax.all_to_all(own_coef, "scen", split_axis=1, concat_axis=0, tiled=True)
    row_width = owned.shape[1] * owned.shape[2]
    coef_rows = owned.reshape(owned_rows, row_width)

    names_all = heard[:, LEG_LANE : LEG_LANE + 2].astype(jnp.int32).reshape(width_trade, leg_total)
    leg_ids = jnp.arange(leg_total, dtype=jnp.int32)
    earlier = leg_ids[None, :] < leg_ids[:, None]
    mine = names_all // owned_rows == trade_at
    local_all = names_all % owned_rows
    rank_here = jnp.sum((mine[:, None, :] & earlier[None]).astype(jnp.int32), axis=2)
    slots = jnp.arange(cap_slots, dtype=jnp.int32)
    hit = mine[:, None, :] & (rank_here[:, None, :] == slots[None, :, None])
    wanted = jnp.sum(jnp.where(hit, local_all[:, None, :], 0), axis=2)
    fetched = coef_rows[wanted]
    draws = path_draws(windows, 0)
    fetched, draws = lax.optimization_barrier((fetched, draws))
    replies = lax.all_to_all(fetched, "trade", split_axis=0, concat_axis=0, tiled=True)
    draws = path_draws(windows, 1, draws)

    rows = replies.reshape(width_trade * cap_slots, row_width)
    values, parts = path_values(rows, terms, book, draws, trades_here, devices)
    parts = lax.all_to_all(parts, everywhere, split_axis=0, concat_axis=0, tiled=True)
    desk_pnl, shortfall = tail(parts)
    return (values.T, desk_pnl, shortfall[0])


def solution(mesh):
    return jax.shard_map(
        per_device,
        mesh=mesh,
        in_specs=(
            P(None, ("trade", "scen"), None),
            P(("trade", "scen"), None),
            P("scen", None),
            P("scen"),
            P("trade", None),
            P("trade"),
            P("trade"),
            P("trade"),
            P("trade"),
            P(),
            P("trade"),
        ),
        out_specs=(P("trade", "scen"), P("scen"), P()),
        check_vma=False,
    )
```

```python
import functools
import math

import jax
import jax.numpy as jnp
import numpy as np
from jax import lax
from jax.experimental import pallas as pl
from jax.experimental.pallas import tpu as pltpu
from jax.sharding import PartitionSpec as P

MAT = 64
COEF = 16
TROWS = 2048
PATHS = 256
ES_TAIL = 4


CORRELATION = 0.6
CORR_COMPLEMENT = 0.8
BARRIER_LOG = -0.35
SMOOTHING = 0.03
COUPON_RATE = 0.08


VOL_LOW = 0.05
VOL_SPAN = 0.225


def power_basis():
    half = COEF // 2
    cheb = np.zeros((half, half))
    cheb[0, 0] = 1.0
    cheb[1, 1] = 1.0
    for k in range(2, half):
        cheb[k, 1:] = 2.0 * cheb[k - 1, :-1]
        cheb[k] -= cheb[k - 2]
    odd = np.zeros((half, half))
    odd[0, 0] = 1.0
    for k in range(1, half):
        odd[k] = 2.0 * cheb[k] - odd[k - 1]
    scale = 2.0 ** np.arange(half)
    conv = np.zeros((COEF, COEF))
    for k in range(half):
        conv[:half, 2 * k] = 0.5 * cheb[k] * scale
        conv[half:, 2 * k + 1] = 0.5 * odd[k] * scale
    return conv


def basis_block():
    return np.kron(np.eye(256 // COEF), power_basis())


def label_rows(names_ref, class_ref, knock_ref, call_ref, kind_ref, book_ref, count_ref, owned_rows, cap_slots):
    trades = knock_ref.shape[0]
    owners = count_ref.shape[0]
    lane = lax.broadcasted_iota(jnp.int32, (1, 128), 1)
    trade_of = lane % trades
    for owner in range(owners):
        count_ref[owner] = 0
    rows = [jnp.zeros((1, 128), jnp.int32)] * 5
    book = jnp.zeros((1, 128), jnp.float32)
    for trade in range(trades):
        here = trade_of == trade
        scalars = [knock_ref[trade], call_ref[trade], kind_ref[trade]]
        for leg in range(2):
            owner = names_ref[leg, trade] // owned_rows
            rank = count_ref[owner]
            count_ref[owner] = rank + 1
            scalars.append(owner * cap_slots + rank)
        rows = [jnp.where(here, x, row) for x, row in zip(scalars, rows)]
        book = jnp.where(here, book_ref[trade], book)
    scen_shift = jnp.where((lane // trades) % 2 == 1, owners * cap_slots, 0)
    rows = rows[:3] + [row + scen_shift for row in rows[3:]]
    class_of = jnp.where(lane == 64, class_ref[0], jnp.where(lane == 65, class_ref[1], -1))
    factor = jnp.zeros((1, 128), jnp.float32)
    for at, weeks in enumerate((1.0, 2.0, 4.0, 6.0, 12.0)):
        factor = jnp.where(class_of == at, math.sqrt(weeks), factor)
    return rows, [book, factor]


def windows_kernel(
    offsets_ref, names_ref, class_ref, knock_ref, call_ref, kind_ref, book_ref, table_ref,
    windows_ref, terms_ref, amounts_ref, first_ref, second_ref, count_ref, *, owned_rows, cap_slots,
):
    rows, amounts = label_rows(
        names_ref, class_ref, knock_ref, call_ref, kind_ref, book_ref, count_ref, owned_rows, cap_slots
    )
    for at, row in enumerate(rows):
        terms_ref[at : at + 1, :] = row
    for at, row in enumerate(amounts):
        amounts_ref[at : at + 1, :] = row
    trades = offsets_ref.shape[0]
    root_step = VOL_SPAN * math.sqrt(1.0 / MAT)
    table = table_ref[...]
    far = jnp.concatenate([table[:, TROWS // 2 :], table[:, : TROWS // 2]], axis=1)
    first = root_step * table
    second = root_step * (CORRELATION * table + CORR_COMPLEMENT * far)
    first_ref[:, :TROWS] = first
    first_ref[:, TROWS:] = first[:, :256]
    second_ref[:, :TROWS] = second
    second_ref[:, TROWS:] = second[:, :256]
    low = lax.broadcasted_iota(jnp.int32, (MAT, 128), 1) < 64

    def one_trade(trade, carry):
        offset = offsets_ref[trade]
        base = pl.multiple_of((offset // 128) * 128, 128)
        shift = offset % 128
        near = first_ref[:, pl.ds(base, 384)]
        other = second_ref[:, pl.ds(base, 384)]
        near_at = pltpu.roll(near, 384 - shift, 1)
        near_up = pltpu.roll(near, 320 - shift, 1)
        other_at = pltpu.roll(other, 384 - shift, 1)
        other_down = pltpu.roll(other, (448 - shift) % 384, 1)
        for half in range(2):
            cut = slice(half * 128, half * 128 + 128)
            even = jnp.where(low, near_at[:, cut], other_down[:, cut])
            odd = jnp.where(low, near_up[:, cut], other_at[:, cut])
            row = pl.multiple_of((2 * half * trades + trade) * MAT, MAT)
            windows_ref[pl.ds(row, MAT), :] = even
            row = pl.multiple_of(((2 * half + 1) * trades + trade) * MAT, MAT)
            windows_ref[pl.ds(row, MAT), :] = odd
        return carry

    lax.fori_loop(0, trades, one_trade, 0)


def path_windows(offsets, names, scen_class, knock, call, kind, book, table, owners, owned_rows, cap_slots):
    trades = offsets.shape[0]
    scalars = pl.BlockSpec(memory_space=pltpu.SMEM)
    vector = pl.BlockSpec(memory_space=pltpu.VMEM)
    return pl.pallas_call(
        functools.partial(windows_kernel, owned_rows=owned_rows, cap_slots=cap_slots),
        out_shape=(
            jax.ShapeDtypeStruct((4 * trades * MAT, 128), jnp.float32),
            jax.ShapeDtypeStruct((16, 128), jnp.int32),
            jax.ShapeDtypeStruct((16, 128), jnp.float32),
        ),
        in_specs=[scalars] * 7 + [vector],
        out_specs=(vector, vector, vector),
        scratch_shapes=[
            pltpu.VMEM((MAT, TROWS + 256), jnp.float32),
            pltpu.VMEM((MAT, TROWS + 256), jnp.float32),
            pltpu.SMEM((owners,), jnp.int32),
        ],
        name="path_windows",
    )(offsets, names, scen_class, knock, call, kind, book, table)


TURN = 8


def turn_kernel(first_step, windows_ref, *refs):
    out_ref = refs[-1]
    groups = windows_ref.shape[0] // MAT
    trades = groups // 4
    start = first_step + pl.program_id(0) * TURN
    for inner in range(TURN):
        rows = windows_ref[pl.ds(start + inner, groups, stride=MAT), :]
        pieces = []
        for group in range(4):
            part = rows[group * trades : (group + 1) * trades]
            pieces += [part, part]
        out_ref[inner] = jnp.concatenate(pieces, axis=0).T


def path_draws(windows, half, earlier=None):
    blocks = MAT // 2 // TURN
    operands = [windows] if earlier is None else [windows, earlier]
    in_specs = [pl.BlockSpec(windows.shape, lambda b: (0, 0)), pl.BlockSpec(memory_space=pl.ANY)]
    return pl.pallas_call(
        lambda *refs: turn_kernel(half * (MAT // 2), *refs),
        grid=(blocks,),
        out_shape=jax.ShapeDtypeStruct((MAT, 128, 128), jnp.float32),
        in_specs=in_specs[: len(operands)],
        out_specs=pl.BlockSpec((TURN, 128, 128), lambda b: (half * blocks + b, 0, 0)),
        input_output_aliases={} if earlier is None else {1: 0},
        name="path_draws",
    )(*operands)


BLOCK = 16
TILES = 4


def spread(ref, row):
    return ref[pl.ds(row, 8, stride=0), :]


def paths_kernel(
    rows_ref, basis_ref, terms_ref, book_ref, draws_ref,
    value_ref, sent_ref, coef_ref, state_ref,
):
    block = pl.program_id(0)

    @pl.when(block == 0)
    def _():
        owners, slots, width = rows_ref.shape
        width //= 2
        whole_rows = rows_ref[...].reshape(owners * slots, 2 * width)
        rows = jnp.concatenate([whole_rows[:, :width], whole_rows[:, width:]], axis=0)
        slot = lax.broadcasted_iota(jnp.int32, (128, 128), 0)
        pick = [jnp.where(slot == terms_ref[3 + leg : 4 + leg, :], 1.0, 0.0) for leg in range(2)]
        pick = jnp.concatenate(pick, axis=1).astype(jnp.bfloat16)
        chosen = lax.dot_general(
            rows, pick, (((0,), (0,)), ((), ())), preferred_element_type=jnp.float32
        ).astype(jnp.bfloat16)
        part = basis_ref.shape[0]
        for at in range(0, width, part):
            terms = jnp.dot(
                basis_ref[...], chosen[at : at + part], preferred_element_type=jnp.float32
            )
            coef_ref[at : at + part, :] = terms[:, :128]
            coef_ref[width + at : width + at + part, :] = terms[:, 128:]
        zeros = jnp.zeros((64, 128), jnp.float32)
        state_ref[0] = zeros
        state_ref[1] = zeros
        state_ref[2] = zeros + 1.0
        state_ref[3] = zeros + 1.0
        state_ref[4] = zeros

    step_size = 1.0 / MAT
    half_count = COEF // 2
    knock_start = spread(terms_ref, 0)
    call_start = spread(terms_ref, 1)
    slope = 0.5 / SMOOTHING
    barrier_shift = -BARRIER_LOG * slope

    def leg_step(logs, leg, step, draw_row):
        row = leg * (MAT * COEF) + step * COEF
        bent = [jnp.tanh(x) for x in logs]
        power = [y * y - 0.5 for y in bent]

        def series(first):
            top = spread(coef_ref, row + first + half_count - 1)
            total = [top] * len(logs)
            for k in range(half_count - 2, -1, -1):
                term = spread(coef_ref, row + first + k)
                total = [s * v + term for s, v in zip(total, power)]
            return total

        even = series(0)
        odd = series(half_count)
        out = []
        for at, x in enumerate(logs):
            vol = VOL_LOW / VOL_SPAN + 1.0 + jnp.tanh(even[at] + bent[at] * odd[at])
            draw = draws_ref[step % BLOCK, pl.ds(draw_row + at * 8, 8), :]
            out.append(x + vol * (draw - (0.5 * step_size * VOL_SPAN**2) * vol))
        return out

    for sweep in range(8 // TILES):
        top_row = sweep * TILES * 8

        def load(at):
            return [state_ref[at, top_row + i * 8 : top_row + i * 8 + 8, :] for i in range(TILES)]

        def one_step(step, state):
            first, second, survival, alive, paid = state
            first = leg_step(first, 0, step, top_row)
            second = leg_step(second, 1, step, 64 + top_row)
            worst = [jnp.minimum(a, b) for a, b in zip(first, second)]
            scaled = [w * slope for w in worst]
            watch = jnp.where(step >= knock_start, barrier_shift, 1e6)
            gap = step - call_start
            seen = (gap >= 0) & ((gap & (MAT // 8 - 1)) == 0) & (step < MAT - 1)
            call = jnp.where(seen, 0.0, -1e6)
            passed = step % BLOCK
            coupon = 1.0 + COUPON_RATE * (step + 1).astype(jnp.float32) / MAT
            coupon = coupon * (1 << (BLOCK - 1 - passed)).astype(jnp.float32) * 2.0**-BLOCK
            survival = [v + v * jnp.tanh(w + watch) for v, w in zip(survival, scaled)]
            part = [a * jnp.tanh(w + call) for a, w in zip(alive, scaled)]
            paid = [p + (a + c) * coupon for p, a, c in zip(paid, alive, part)]
            alive = [a - c for a, c in zip(alive, part)]
            return (first, second, survival, alive, paid)

        def some_steps(at, state):
            for inner in range(UNROLL):
                state = one_step(block * BLOCK + at * UNROLL + inner, state)
            return state

        state = tuple(load(at) for at in range(5))
        state = lax.fori_loop(0, BLOCK // UNROLL, some_steps, state)
        for at in range(5):
            for i in range(TILES):
                value = state[at][i] * 2.0**-BLOCK if at in (2, 3) else state[at][i]
                state_ref[at, top_row + i * 8 : top_row + i * 8 + 8, :] = value

    @pl.when(block == MAT // BLOCK - 1)
    def _():
        worst = jnp.minimum(state_ref[0], state_ref[1])
        knocked = 1.0 - state_ref[2]
        growth = jnp.exp(worst)
        note = state_ref[4] + state_ref[3] * (1.0 + knocked * jnp.minimum(growth - 1.0, 0.0))
        put = knocked * jnp.maximum(1.0 - growth, 0.0)
        payoff = jnp.where(terms_ref[2:3, :] == 0, note, put)
        total = jnp.sum(payoff, axis=0, keepdims=True)
        total = jnp.broadcast_to(total, (8, 128))
        total = total + pltpu.roll(total, 64, 1)
        total = total + pltpu.roll(total, 32, 1)
        total = total * (1.0 / PATHS)
        trades = value_ref.shape[1]
        value_ref[0:1, :] = total[0:1, :trades]
        value_ref[1:2, :] = pltpu.roll(total, 128 - trades, 1)[0:1, :trades]
        gain = total - spread(book_ref, 0)
        shift = trades // 2
        while shift:
            gain = gain + pltpu.roll(gain, shift, 1)
            shift //= 2
        lane = lax.broadcasted_iota(jnp.int32, (8, 128), 1)
        sent = spread(book_ref, 1)
        sent = jnp.where(lane == 0, pltpu.roll(gain, 129 - trades, 1), sent)
        sent = jnp.where(lane == 1, pltpu.roll(gain, 130 - 2 * trades, 1), sent)
        sent_ref[...] = jnp.broadcast_to(sent[0:1, :], sent_ref.shape)


UNROLL = 8


def path_values(rows, terms, book, draws, trades, devices):
    whole = lambda *dims: pl.BlockSpec(dims, lambda b: (0,) * len(dims))
    return pl.pallas_call(
        paths_kernel,
        grid=(MAT // BLOCK,),
        out_shape=(
            jax.ShapeDtypeStruct((2, trades), jnp.float32),
            jax.ShapeDtypeStruct((devices, 128), jnp.float32),
        ),
        in_specs=[
            whole(*rows.shape),
            whole(256, 256),
            whole(*terms.shape),
            whole(*book.shape),
            pl.BlockSpec((BLOCK, 128, 128), lambda b: (b, 0, 0)),
        ],
        out_specs=(whole(2, trades), whole(devices, 128)),
        scratch_shapes=[
            pltpu.VMEM((2 * MAT * COEF + 8, 128), jnp.float32),
            pltpu.VMEM((5, 64, 128), jnp.float32),
        ],
        name="path_values",
    )(rows, jnp.asarray(basis_block(), jnp.bfloat16), terms, book, draws)


SLICE = 16
LEG_LANE = 2 * SLICE


def pack_kernel(names_ref, class_ref, shocks_ref, out_ref, wide_ref):
    trade_at = lax.axis_index("trade")
    scen_at = lax.axis_index("scen")
    factors = shocks_ref.shape[1]
    wide = wide_ref.shape[1]
    wide_ref[...] = jnp.zeros(wide_ref.shape, jnp.float32)
    wide_ref[0:2, :factors] = shocks_ref[...]
    row = lax.broadcasted_iota(jnp.int32, wide_ref.shape, 0)
    lane = lax.broadcasted_iota(jnp.int32, wide_ref.shape, 1)
    class_of = jnp.where(row == 0, class_ref[0], class_ref[1])
    masked = jnp.where(lane * 5 >= class_of * factors, wide_ref[...], 0.0)
    here = pltpu.roll(masked, (wide - trade_at * SLICE) % wide, 1)[:, :128]
    after = pltpu.roll(here, SLICE, 1)
    lane = lax.broadcasted_iota(jnp.int32, (1, 128), 1)
    sent = jnp.where(lane < SLICE, here[0:1, :], after[1:2, :])
    for leg in range(2):
        name = names_ref[leg, scen_at].astype(jnp.float32)
        sent = jnp.where(lane == LEG_LANE + leg, name, sent)
    out_ref[...] = jnp.broadcast_to(sent, out_ref.shape)


def pack(names, scen_class, shocks, devices):
    return pl.pallas_call(
        pack_kernel,
        out_shape=jax.ShapeDtypeStruct((devices, 128), jnp.float32),
        in_specs=[
            pl.BlockSpec(memory_space=pltpu.SMEM),
            pl.BlockSpec(memory_space=pltpu.SMEM),
            pl.BlockSpec(memory_space=pltpu.VMEM),
        ],
        out_specs=pl.BlockSpec(memory_space=pltpu.VMEM),
        scratch_shapes=[pltpu.VMEM((8, 256), jnp.float32)],
        name="pack",
    )(names, scen_class, shocks)


def unpack_kernel(heard_ref, out_ref, rows_ref):
    scens = out_ref.shape[0] // 2
    lane = lax.broadcasted_iota(jnp.int32, (scens, 128), 1)
    per_tile = 128 // SLICE
    for tile in range(2):
        for scen in range(2):
            total = jnp.zeros((scens, 128), jnp.float32)
            for at in range(per_tile):
                first = (tile * per_tile + at) * scens
                part = heard_ref[first : first + scens, :]
                part = pltpu.roll(part, ((at - scen) * SLICE) % 128, 1)
                total = jnp.where(lane // SLICE == at, part, total)
            rows_ref[pl.ds(tile * 2 * scens + scen, scens, stride=2), :] = total
    out_ref[:, :128] = rows_ref[: 2 * scens, :].astype(jnp.bfloat16)
    out_ref[:, 128:] = rows_ref[2 * scens :, : out_ref.shape[1] - 128].astype(jnp.bfloat16)


def unpack(heard, scens, factors):
    return pl.pallas_call(
        unpack_kernel,
        out_shape=jax.ShapeDtypeStruct((2 * scens, factors), jnp.bfloat16),
        in_specs=[pl.BlockSpec(memory_space=pltpu.VMEM)],
        out_specs=pl.BlockSpec(memory_space=pltpu.VMEM),
        scratch_shapes=[pltpu.VMEM((4 * scens, 128), jnp.float32)],
        name="unpack",
    )(heard)


def tail_kernel(heard_ref, desk_ref, tail_ref):
    scen_at = lax.axis_index("scen")
    scens = lax.axis_size("scen")
    blocks = heard_ref.shape[0] // scens
    total = heard_ref[0:scens, :]
    factor = pltpu.roll(total, 64, 1)
    for block in range(1, blocks):
        total = total + heard_ref[block * scens : (block + 1) * scens, :]
    pnl = total / math.sqrt(blocks * 16)
    row = lax.broadcasted_iota(jnp.int32, (scens, 128), 0)
    lane = lax.broadcasted_iota(jnp.int32, (scens, 128), 1)
    loss = -pnl * factor
    turned = jnp.concatenate([loss] * (128 // scens), axis=0).T
    other = lane % scens
    picked = jnp.zeros((1, 128), jnp.float32)
    for scen in range(2):
        mine = turned[scen : scen + 1, :]
        above = jnp.zeros((scens, 128), jnp.float32)
        for rival in range(2):
            theirs = jnp.broadcast_to(loss[:, rival : rival + 1], (scens, 128))
            first = 2 * row + rival < 2 * other + scen
            above = above + jnp.where((theirs > mine) | ((theirs == mine) & first), 1.0, 0.0)
        rank = jnp.sum(above, axis=0, keepdims=True)
        picked = picked + jnp.where((rank < ES_TAIL) & (lane[0:1] < scens), mine, 0.0)
    tail_ref[0] = jnp.sum(picked) * (1.0 / ES_TAIL)
    for scen in range(2):
        desk_ref[scen] = jnp.sum(jnp.where((row == scen_at) & (lane == scen), pnl, 0.0))


def tail(heard):
    return pl.pallas_call(
        tail_kernel,
        out_shape=(
            jax.ShapeDtypeStruct((2,), jnp.float32),
            jax.ShapeDtypeStruct((1,), jnp.float32),
        ),
        in_specs=[pl.BlockSpec(memory_space=pltpu.VMEM)],
        out_specs=(
            pl.BlockSpec(memory_space=pltpu.SMEM),
            pl.BlockSpec(memory_space=pltpu.SMEM),
        ),
        name="tail",
    )(heard)


def per_device(
    loadings,
    base_coef,
    shocks,
    scen_class,
    names,
    trade_kind,
    call_start,
    knock_start,
    offsets,
    normal_table,
    book_value,
):
    factors = shocks.shape[1]
    scen_here = shocks.shape[0]
    trades_here = names.shape[0]
    width_trade = lax.axis_size("trade")
    width_scen = lax.axis_size("scen")
    trade_at = lax.axis_index("trade")
    everywhere = ("trade", "scen")
    devices = width_trade * width_scen
    owned_rows = base_coef.shape[0] * width_scen
    cap_slots = max(2, (4 * trades_here + width_trade - 1) // width_trade)
    leg_total = 2 * trades_here

    sent = pack(names.T, scen_class, shocks, devices)
    heard = lax.all_to_all(sent, everywhere, split_axis=0, concat_axis=0, tiled=True)
    everyone = unpack(heard, width_scen, factors)
    product = jnp.einsum("sf,fum->usm", everyone, loadings, preferred_element_type=jnp.float32)
    own_coef = (product + base_coef[:, None, :].astype(jnp.float32)).astype(jnp.bfloat16)
    windows, terms, book = path_windows(
        offsets, names.T, scen_class, knock_start, call_start, trade_kind, book_value,
        normal_table, width_trade, owned_rows, cap_slots,
    )
    own_coef, windows, heard = lax.optimization_barrier((own_coef, windows, heard))
    owned = lax.all_to_all(own_coef, "scen", split_axis=1, concat_axis=0, tiled=True)
    row_width = owned.shape[1] * owned.shape[2]
    coef_rows = owned.reshape(owned_rows, row_width)

    names_all = heard[:, LEG_LANE : LEG_LANE + 2].astype(jnp.int32).reshape(width_trade, leg_total)
    leg_ids = jnp.arange(leg_total, dtype=jnp.int32)
    earlier = leg_ids[None, :] < leg_ids[:, None]
    mine = names_all // owned_rows == trade_at
    local_all = names_all % owned_rows
    rank_here = jnp.sum((mine[:, None, :] & earlier[None]).astype(jnp.int32), axis=2)
    slots = jnp.arange(cap_slots, dtype=jnp.int32)
    hit = mine[:, None, :] & (rank_here[:, None, :] == slots[None, :, None])
    wanted = jnp.sum(jnp.where(hit, local_all[:, None, :], 0), axis=2)
    fetched = coef_rows[wanted]
    draws = path_draws(windows, 0)
    fetched, draws = lax.optimization_barrier((fetched, draws))
    replies = lax.all_to_all(fetched, "trade", split_axis=0, concat_axis=0, tiled=True)
    draws = path_draws(windows, 1, draws)

    values, parts = path_values(replies, terms, book, draws, trades_here, devices)
    parts = lax.all_to_all(parts, everywhere, split_axis=0, concat_axis=0, tiled=True)
    desk_pnl, shortfall = tail(parts)
    return (values.T, desk_pnl, shortfall[0])


def solution(mesh):
    return jax.shard_map(
        per_device,
        mesh=mesh,
        in_specs=(
            P(None, ("trade", "scen"), None),
            P(("trade", "scen"), None),
            P("scen", None),
            P("scen"),
            P("trade", None),
            P("trade"),
            P("trade"),
            P("trade"),
            P("trade"),
            P(),
            P("trade"),
        ),
        out_specs=(P("trade", "scen"), P("scen"), P()),
        check_vma=False,
    )
```

```python
import functools
import math

import jax
import jax.numpy as jnp
import numpy as np
from jax import lax
from jax.experimental import pallas as pl
from jax.experimental.pallas import tpu as pltpu
from jax.sharding import PartitionSpec as P

MAT = 64
COEF = 16
TROWS = 2048
PATHS = 256
ES_TAIL = 4


CORRELATION = 0.6
CORR_COMPLEMENT = 0.8
BARRIER_LOG = -0.35
SMOOTHING = 0.03
COUPON_RATE = 0.08


VOL_LOW = 0.05
VOL_SPAN = 0.225


def power_basis():
    half = COEF // 2
    cheb = np.zeros((half, half))
    cheb[0, 0] = 1.0
    cheb[1, 1] = 1.0
    for k in range(2, half):
        cheb[k, 1:] = 2.0 * cheb[k - 1, :-1]
        cheb[k] -= cheb[k - 2]
    odd = np.zeros((half, half))
    odd[0, 0] = 1.0
    for k in range(1, half):
        odd[k] = 2.0 * cheb[k] - odd[k - 1]
    scale = 2.0 ** np.arange(half)
    conv = np.zeros((COEF, COEF))
    for k in range(half):
        conv[:half, 2 * k] = 0.5 * cheb[k] * scale
        conv[half:, 2 * k + 1] = 0.5 * odd[k] * scale
    return conv


def basis_block():
    return np.kron(np.eye(256 // COEF), power_basis())


def label_rows(names_ref, class_ref, knock_ref, call_ref, kind_ref, book_ref, count_ref, owned_rows, cap_slots):
    trades = knock_ref.shape[0]
    owners = count_ref.shape[0]
    lane = lax.broadcasted_iota(jnp.int32, (1, 128), 1)
    trade_of = lane % trades
    for owner in range(owners):
        count_ref[owner] = 0
    rows = [jnp.zeros((1, 128), jnp.int32)] * 5
    book = jnp.zeros((1, 128), jnp.float32)
    for trade in range(trades):
        here = trade_of == trade
        scalars = [knock_ref[trade], call_ref[trade], kind_ref[trade]]
        for leg in range(2):
            owner = names_ref[leg, trade] // owned_rows
            rank = count_ref[owner]
            count_ref[owner] = rank + 1
            scalars.append(owner * cap_slots + rank)
        rows = [jnp.where(here, x, row) for x, row in zip(scalars, rows)]
        book = jnp.where(here, book_ref[trade], book)
    scen_shift = jnp.where((lane // trades) % 2 == 1, owners * cap_slots, 0)
    rows = rows[:3] + [row + scen_shift for row in rows[3:]]
    class_of = jnp.where(lane == 64, class_ref[0], jnp.where(lane == 65, class_ref[1], -1))
    factor = jnp.zeros((1, 128), jnp.float32)
    for at, weeks in enumerate((1.0, 2.0, 4.0, 6.0, 12.0)):
        factor = jnp.where(class_of == at, math.sqrt(weeks), factor)
    return rows, [book, factor]


def windows_kernel(
    offsets_ref, names_ref, class_ref, knock_ref, call_ref, kind_ref, book_ref, table_ref,
    windows_ref, terms_ref, amounts_ref, first_ref, second_ref, count_ref, *, owned_rows, cap_slots,
):
    rows, amounts = label_rows(
        names_ref, class_ref, knock_ref, call_ref, kind_ref, book_ref, count_ref, owned_rows, cap_slots
    )
    for at, row in enumerate(rows):
        terms_ref[at : at + 1, :] = row
    for at, row in enumerate(amounts):
        amounts_ref[at : at + 1, :] = row
    trades = offsets_ref.shape[0]
    root_step = VOL_SPAN * math.sqrt(1.0 / MAT)
    table = table_ref[...]
    far = jnp.concatenate([table[:, TROWS // 2 :], table[:, : TROWS // 2]], axis=1)
    first = root_step * table
    second = root_step * (CORRELATION * table + CORR_COMPLEMENT * far)
    first_ref[:, :TROWS] = first
    first_ref[:, TROWS:] = first[:, :256]
    second_ref[:, :TROWS] = second
    second_ref[:, TROWS:] = second[:, :256]
    low = lax.broadcasted_iota(jnp.int32, (MAT, 128), 1) < 64

    def one_trade(trade, carry):
        offset = offsets_ref[trade]
        base = pl.multiple_of((offset // 128) * 128, 128)
        shift = offset % 128
        near = first_ref[:, pl.ds(base, 384)]
        other = second_ref[:, pl.ds(base, 384)]
        near_at = pltpu.roll(near, 384 - shift, 1)
        near_up = pltpu.roll(near, 320 - shift, 1)
        other_at = pltpu.roll(other, 384 - shift, 1)
        other_down = pltpu.roll(other, (448 - shift) % 384, 1)
        for half in range(2):
            cut = slice(half * 128, half * 128 + 128)
            even = jnp.where(low, near_at[:, cut], other_down[:, cut])
            odd = jnp.where(low, near_up[:, cut], other_at[:, cut])
            row = pl.multiple_of((2 * half * trades + trade) * MAT, MAT)
            windows_ref[pl.ds(row, MAT), :] = even
            row = pl.multiple_of(((2 * half + 1) * trades + trade) * MAT, MAT)
            windows_ref[pl.ds(row, MAT), :] = odd
        return carry

    lax.fori_loop(0, trades, one_trade, 0)


def path_windows(offsets, names, scen_class, knock, call, kind, book, table, owners, owned_rows, cap_slots):
    trades = offsets.shape[0]
    scalars = pl.BlockSpec(memory_space=pltpu.SMEM)
    vector = pl.BlockSpec(memory_space=pltpu.VMEM)
    return pl.pallas_call(
        functools.partial(windows_kernel, owned_rows=owned_rows, cap_slots=cap_slots),
        out_shape=(
            jax.ShapeDtypeStruct((4 * trades * MAT, 128), jnp.float32),
            jax.ShapeDtypeStruct((16, 128), jnp.int32),
            jax.ShapeDtypeStruct((16, 128), jnp.float32),
        ),
        in_specs=[scalars] * 7 + [vector],
        out_specs=(vector, vector, vector),
        scratch_shapes=[
            pltpu.VMEM((MAT, TROWS + 256), jnp.float32),
            pltpu.VMEM((MAT, TROWS + 256), jnp.float32),
            pltpu.SMEM((owners,), jnp.int32),
        ],
        name="path_windows",
    )(offsets, names, scen_class, knock, call, kind, book, table)


TURN = 8


def turn_kernel(first_step, windows_ref, *refs):
    out_ref = refs[-1]
    groups = windows_ref.shape[0] // MAT
    trades = groups // 4
    start = first_step + pl.program_id(0) * TURN
    for inner in range(TURN):
        rows = windows_ref[pl.ds(start + inner, groups, stride=MAT), :]
        pieces = []
        for group in range(4):
            part = rows[group * trades : (group + 1) * trades]
            pieces += [part, part]
        out_ref[inner] = jnp.concatenate(pieces, axis=0).T


def path_draws(windows, half, earlier=None):
    blocks = MAT // 2 // TURN
    operands = [windows] if earlier is None else [windows, earlier]
    in_specs = [pl.BlockSpec(windows.shape, lambda b: (0, 0)), pl.BlockSpec(memory_space=pl.ANY)]
    return pl.pallas_call(
        lambda *refs: turn_kernel(half * (MAT // 2), *refs),
        grid=(blocks,),
        out_shape=jax.ShapeDtypeStruct((MAT, 128, 128), jnp.float32),
        in_specs=in_specs[: len(operands)],
        out_specs=pl.BlockSpec((TURN, 128, 128), lambda b: (half * blocks + b, 0, 0)),
        input_output_aliases={} if earlier is None else {1: 0},
        name="path_draws",
    )(*operands)


BLOCK = 16
TILES = 4


def spread(ref, row):
    return ref[pl.ds(row, 8, stride=0), :]


def paths_kernel(
    rows_ref, basis_ref, terms_ref, book_ref, draws_ref,
    value_ref, sent_ref, coef_ref, state_ref,
):
    block = pl.program_id(0)

    @pl.when(block == 0)
    def _():
        owners, slots, width = rows_ref.shape
        width //= 2
        whole_rows = rows_ref[...].reshape(owners * slots, 2 * width)
        rows = jnp.concatenate([whole_rows[:, :width], whole_rows[:, width:]], axis=0)
        slot = lax.broadcasted_iota(jnp.int32, (128, 128), 0)
        pick = [jnp.where(slot == terms_ref[3 + leg : 4 + leg, :], 1.0, 0.0) for leg in range(2)]
        pick = jnp.concatenate(pick, axis=1).astype(jnp.bfloat16)
        chosen = lax.dot_general(
            rows, pick, (((0,), (0,)), ((), ())), preferred_element_type=jnp.float32
        ).astype(jnp.bfloat16)
        part = basis_ref.shape[0]
        for at in range(0, width, part):
            terms = jnp.dot(
                basis_ref[...], chosen[at : at + part], preferred_element_type=jnp.float32
            )
            coef_ref[at : at + part, :] = terms[:, :128]
            coef_ref[width + at : width + at + part, :] = terms[:, 128:]
        zeros = jnp.zeros((64, 128), jnp.float32)
        state_ref[0] = zeros
        state_ref[1] = zeros
        state_ref[2] = zeros + 1.0
        state_ref[3] = zeros + 1.0
        state_ref[4] = zeros

    step_size = 1.0 / MAT
    half_count = COEF // 2
    knock_start = spread(terms_ref, 0)
    call_start = spread(terms_ref, 1)
    slope = 0.5 / SMOOTHING
    barrier_shift = -BARRIER_LOG * slope

    def leg_step(logs, leg, step, draw_row):
        row = leg * (MAT * COEF) + step * COEF
        bent = [jnp.tanh(x) for x in logs]
        power = [y * y - 0.5 for y in bent]

        def series(first):
            top = spread(coef_ref, row + first + half_count - 1)
            total = [top] * len(logs)
            for k in range(half_count - 2, -1, -1):
                term = spread(coef_ref, row + first + k)
                total = [s * v + term for s, v in zip(total, power)]
            return total

        even = series(0)
        odd = series(half_count)
        out = []
        for at, x in enumerate(logs):
            vol = VOL_LOW / VOL_SPAN + 1.0 + jnp.tanh(even[at] + bent[at] * odd[at])
            draw = draws_ref[step % BLOCK, pl.ds(draw_row + at * 8, 8), :]
            out.append(x + vol * (draw - (0.5 * step_size * VOL_SPAN**2) * vol))
        return out

    for sweep in range(8 // TILES):
        top_row = sweep * TILES * 8

        def load(at):
            return [state_ref[at, top_row + i * 8 : top_row + i * 8 + 8, :] for i in range(TILES)]

        def one_step(step, state):
            first, second, survival, alive, paid = state
            first = leg_step(first, 0, step, top_row)
            second = leg_step(second, 1, step, 64 + top_row)
            worst = [jnp.minimum(a, b) for a, b in zip(first, second)]
            scaled = [w * slope for w in worst]
            watch = jnp.where(step >= knock_start, barrier_shift, 1e6)
            gap = step - call_start
            seen = (gap >= 0) & ((gap & (MAT // 8 - 1)) == 0) & (step < MAT - 1)
            call = jnp.where(seen, 0.0, -1e6)
            passed = step % BLOCK
            coupon = 1.0 + COUPON_RATE * (step + 1).astype(jnp.float32) / MAT
            coupon = coupon * (1 << (BLOCK - 1 - passed)).astype(jnp.float32) * 2.0**-BLOCK
            survival = [v + v * jnp.tanh(w + watch) for v, w in zip(survival, scaled)]
            part = [a * jnp.tanh(w + call) for a, w in zip(alive, scaled)]
            paid = [p + (a + c) * coupon for p, a, c in zip(paid, alive, part)]
            alive = [a - c for a, c in zip(alive, part)]
            return (first, second, survival, alive, paid)

        def some_steps(at, state):
            for inner in range(UNROLL):
                state = one_step(block * BLOCK + at * UNROLL + inner, state)
            return state

        state = tuple(load(at) for at in range(5))
        state = lax.fori_loop(0, BLOCK // UNROLL, some_steps, state)
        for at in range(5):
            for i in range(TILES):
                value = state[at][i] * 2.0**-BLOCK if at in (2, 3) else state[at][i]
                state_ref[at, top_row + i * 8 : top_row + i * 8 + 8, :] = value

    @pl.when(block == MAT // BLOCK - 1)
    def _():
        worst = jnp.minimum(state_ref[0], state_ref[1])
        knocked = 1.0 - state_ref[2]
        growth = jnp.exp(worst)
        note = state_ref[4] + state_ref[3] * (1.0 + knocked * jnp.minimum(growth - 1.0, 0.0))
        put = knocked * jnp.maximum(1.0 - growth, 0.0)
        payoff = jnp.where(terms_ref[2:3, :] == 0, note, put)
        total = jnp.sum(payoff, axis=0, keepdims=True)
        total = jnp.broadcast_to(total, (8, 128))
        total = total + pltpu.roll(total, 64, 1)
        total = total + pltpu.roll(total, 32, 1)
        total = total * (1.0 / PATHS)
        trades = value_ref.shape[1]
        value_ref[0:1, :] = total[0:1, :trades]
        value_ref[1:2, :] = pltpu.roll(total, 128 - trades, 1)[0:1, :trades]
        gain = total - spread(book_ref, 0)
        shift = trades // 2
        while shift:
            gain = gain + pltpu.roll(gain, shift, 1)
            shift //= 2
        lane = lax.broadcasted_iota(jnp.int32, (8, 128), 1)
        sent = spread(book_ref, 1)
        sent = jnp.where(lane == 0, pltpu.roll(gain, 129 - trades, 1), sent)
        sent = jnp.where(lane == 1, pltpu.roll(gain, 130 - 2 * trades, 1), sent)
        sent_ref[...] = jnp.broadcast_to(sent[0:1, :], sent_ref.shape)


UNROLL = 16


def path_values(rows, terms, book, draws, trades, devices):
    whole = lambda *dims: pl.BlockSpec(dims, lambda b: (0,) * len(dims))
    return pl.pallas_call(
        paths_kernel,
        grid=(MAT // BLOCK,),
        out_shape=(
            jax.ShapeDtypeStruct((2, trades), jnp.float32),
            jax.ShapeDtypeStruct((devices, 128), jnp.float32),
        ),
        in_specs=[
            whole(*rows.shape),
            whole(256, 256),
            whole(*terms.shape),
            whole(*book.shape),
            pl.BlockSpec((BLOCK, 128, 128), lambda b: (b, 0, 0)),
        ],
        out_specs=(whole(2, trades), whole(devices, 128)),
        scratch_shapes=[
            pltpu.VMEM((2 * MAT * COEF + 8, 128), jnp.float32),
            pltpu.VMEM((5, 64, 128), jnp.float32),
        ],
        name="path_values",
    )(rows, jnp.asarray(basis_block(), jnp.bfloat16), terms, book, draws)


SLICE = 16
LEG_LANE = 2 * SLICE


def pack_kernel(names_ref, class_ref, shocks_ref, out_ref, wide_ref):
    trade_at = lax.axis_index("trade")
    scen_at = lax.axis_index("scen")
    factors = shocks_ref.shape[1]
    wide = wide_ref.shape[1]
    wide_ref[...] = jnp.zeros(wide_ref.shape, jnp.float32)
    wide_ref[0:2, :factors] = shocks_ref[...]
    row = lax.broadcasted_iota(jnp.int32, wide_ref.shape, 0)
    lane = lax.broadcasted_iota(jnp.int32, wide_ref.shape, 1)
    class_of = jnp.where(row == 0, class_ref[0], class_ref[1])
    masked = jnp.where(lane * 5 >= class_of * factors, wide_ref[...], 0.0)
    here = pltpu.roll(masked, (wide - trade_at * SLICE) % wide, 1)[:, :128]
    after = pltpu.roll(here, SLICE, 1)
    lane = lax.broadcasted_iota(jnp.int32, (1, 128), 1)
    sent = jnp.where(lane < SLICE, here[0:1, :], after[1:2, :])
    for leg in range(2):
        name = names_ref[leg, scen_at].astype(jnp.float32)
        sent = jnp.where(lane == LEG_LANE + leg, name, sent)
    out_ref[...] = jnp.broadcast_to(sent, out_ref.shape)


def pack(names, scen_class, shocks, devices):
    return pl.pallas_call(
        pack_kernel,
        out_shape=jax.ShapeDtypeStruct((devices, 128), jnp.float32),
        in_specs=[
            pl.BlockSpec(memory_space=pltpu.SMEM),
            pl.BlockSpec(memory_space=pltpu.SMEM),
            pl.BlockSpec(memory_space=pltpu.VMEM),
        ],
        out_specs=pl.BlockSpec(memory_space=pltpu.VMEM),
        scratch_shapes=[pltpu.VMEM((8, 256), jnp.float32)],
        name="pack",
    )(names, scen_class, shocks)


def unpack_kernel(heard_ref, out_ref, rows_ref):
    scens = out_ref.shape[0] // 2
    lane = lax.broadcasted_iota(jnp.int32, (scens, 128), 1)
    per_tile = 128 // SLICE
    for tile in range(2):
        for scen in range(2):
            total = jnp.zeros((scens, 128), jnp.float32)
            for at in range(per_tile):
                first = (tile * per_tile + at) * scens
                part = heard_ref[first : first + scens, :]
                part = pltpu.roll(part, ((at - scen) * SLICE) % 128, 1)
                total = jnp.where(lane // SLICE == at, part, total)
            rows_ref[pl.ds(tile * 2 * scens + scen, scens, stride=2), :] = total
    out_ref[:, :128] = rows_ref[: 2 * scens, :].astype(jnp.bfloat16)
    out_ref[:, 128:] = rows_ref[2 * scens :, : out_ref.shape[1] - 128].astype(jnp.bfloat16)


def unpack(heard, scens, factors):
    return pl.pallas_call(
        unpack_kernel,
        out_shape=jax.ShapeDtypeStruct((2 * scens, factors), jnp.bfloat16),
        in_specs=[pl.BlockSpec(memory_space=pltpu.VMEM)],
        out_specs=pl.BlockSpec(memory_space=pltpu.VMEM),
        scratch_shapes=[pltpu.VMEM((4 * scens, 128), jnp.float32)],
        name="unpack",
    )(heard)


def tail_kernel(heard_ref, desk_ref, tail_ref):
    scen_at = lax.axis_index("scen")
    scens = lax.axis_size("scen")
    blocks = heard_ref.shape[0] // scens
    total = heard_ref[0:scens, :]
    factor = pltpu.roll(total, 64, 1)
    for block in range(1, blocks):
        total = total + heard_ref[block * scens : (block + 1) * scens, :]
    pnl = total / math.sqrt(blocks * 16)
    row = lax.broadcasted_iota(jnp.int32, (scens, 128), 0)
    lane = lax.broadcasted_iota(jnp.int32, (scens, 128), 1)
    loss = -pnl * factor
    turned = jnp.concatenate([loss] * (128 // scens), axis=0).T
    other = lane % scens
    picked = jnp.zeros((1, 128), jnp.float32)
    for scen in range(2):
        mine = turned[scen : scen + 1, :]
        above = jnp.zeros((scens, 128), jnp.float32)
        for rival in range(2):
            theirs = jnp.broadcast_to(loss[:, rival : rival + 1], (scens, 128))
            first = 2 * row + rival < 2 * other + scen
            above = above + jnp.where((theirs > mine) | ((theirs == mine) & first), 1.0, 0.0)
        rank = jnp.sum(above, axis=0, keepdims=True)
        picked = picked + jnp.where((rank < ES_TAIL) & (lane[0:1] < scens), mine, 0.0)
    tail_ref[0] = jnp.sum(picked) * (1.0 / ES_TAIL)
    for scen in range(2):
        desk_ref[scen] = jnp.sum(jnp.where((row == scen_at) & (lane == scen), pnl, 0.0))


def tail(heard):
    return pl.pallas_call(
        tail_kernel,
        out_shape=(
            jax.ShapeDtypeStruct((2,), jnp.float32),
            jax.ShapeDtypeStruct((1,), jnp.float32),
        ),
        in_specs=[pl.BlockSpec(memory_space=pltpu.VMEM)],
        out_specs=(
            pl.BlockSpec(memory_space=pltpu.SMEM),
            pl.BlockSpec(memory_space=pltpu.SMEM),
        ),
        name="tail",
    )(heard)


def per_device(
    loadings,
    base_coef,
    shocks,
    scen_class,
    names,
    trade_kind,
    call_start,
    knock_start,
    offsets,
    normal_table,
    book_value,
):
    factors = shocks.shape[1]
    scen_here = shocks.shape[0]
    trades_here = names.shape[0]
    width_trade = lax.axis_size("trade")
    width_scen = lax.axis_size("scen")
    trade_at = lax.axis_index("trade")
    everywhere = ("trade", "scen")
    devices = width_trade * width_scen
    owned_rows = base_coef.shape[0] * width_scen
    cap_slots = max(2, (4 * trades_here + width_trade - 1) // width_trade)
    leg_total = 2 * trades_here

    sent = pack(names.T, scen_class, shocks, devices)
    heard = lax.all_to_all(sent, everywhere, split_axis=0, concat_axis=0, tiled=True)
    everyone = unpack(heard, width_scen, factors)
    product = jnp.einsum("sf,fum->usm", everyone, loadings, preferred_element_type=jnp.float32)
    own_coef = (product + base_coef[:, None, :].astype(jnp.float32)).astype(jnp.bfloat16)
    windows, terms, book = path_windows(
        offsets, names.T, scen_class, knock_start, call_start, trade_kind, book_value,
        normal_table, width_trade, owned_rows, cap_slots,
    )
    own_coef, windows, heard = lax.optimization_barrier((own_coef, windows, heard))
    owned = lax.all_to_all(own_coef, "scen", split_axis=1, concat_axis=0, tiled=True)
    row_width = owned.shape[1] * owned.shape[2]
    coef_rows = owned.reshape(owned_rows, row_width)

    names_all = heard[:, LEG_LANE : LEG_LANE + 2].astype(jnp.int32).reshape(width_trade, leg_total)
    leg_ids = jnp.arange(leg_total, dtype=jnp.int32)
    earlier = leg_ids[None, :] < leg_ids[:, None]
    mine = names_all // owned_rows == trade_at
    local_all = names_all % owned_rows
    rank_here = jnp.sum((mine[:, None, :] & earlier[None]).astype(jnp.int32), axis=2)
    slots = jnp.arange(cap_slots, dtype=jnp.int32)
    hit = mine[:, None, :] & (rank_here[:, None, :] == slots[None, :, None])
    wanted = jnp.sum(jnp.where(hit, local_all[:, None, :], 0), axis=2)
    fetched = coef_rows[wanted]
    draws = path_draws(windows, 0)
    fetched, draws = lax.optimization_barrier((fetched, draws))
    replies = lax.all_to_all(fetched, "trade", split_axis=0, concat_axis=0, tiled=True)
    draws = path_draws(windows, 1, draws)

    values, parts = path_values(replies, terms, book, draws, trades_here, devices)
    parts = lax.all_to_all(parts, everywhere, split_axis=0, concat_axis=0, tiled=True)
    desk_pnl, shortfall = tail(parts)
    return (values.T, desk_pnl, shortfall[0])


def solution(mesh):
    return jax.shard_map(
        per_device,
        mesh=mesh,
        in_specs=(
            P(None, ("trade", "scen"), None),
            P(("trade", "scen"), None),
            P("scen", None),
            P("scen"),
            P("trade", None),
            P("trade"),
            P("trade"),
            P("trade"),
            P("trade"),
            P(),
            P("trade"),
        ),
        out_specs=(P("trade", "scen"), P("scen"), P()),
        check_vma=False,
    )
```
